32 devices in a mesh: srv: 8 (over y, x, core), head: 4 (over z).
Axes of the slice: x: 2, y: 2, z: 4, core: 2. Of those that a mesh axis runs over, the one named last changes fastest.
Arguments:
- queries: bfloat16 [2048, 8192], P('srv', 'head'), may hold values from -200 to 200
- key_value_pair: bfloat16 [2, 2048, 1024], P(None, 'srv', 'head'), may hold values from -200 to 200
- lengths: int32 [8], replicated, may hold values from 1 to 1024, 2048 in all
Outputs:
- attended: bfloat16 [2048, 8192], P(('srv', 'head'))
The draws below stay inside these ranges and needn't reach their ends.
All inputs are finite; a program needn't handle non-finite values.
Results may differ from the reference program's by a relative error of at most 0.012.
Values may be sent and summed in bfloat16 or wider, within the bound.
A program may use at most 64 MiB of HBM per device.

```python
import math
import jax
import jax.numpy as jnp
import numpy as np
from jax import lax

HQ = 64
KEY_VALUE_HEADS = 8
HEAD_SIZE = 128
TOK_DEV = 256
NDOC = 8
QUERY_PER_KV = 8
SEQUENCE_TOKENS = 2048
LONGEST = 1024
N_SRV = 8


def activations(key):
    base_key = jax.random.fold_in(key, 7)
    key_sample, value_sample, query_sample = jax.random.split(base_key, 3)
    key_rows = jnp.clip(jax.random.normal(key_sample, (SEQUENCE_TOKENS, KEY_VALUE_HEADS, HEAD_SIZE), jnp.float32), -5.0, 5.0)
    value_rows = jnp.clip(jax.random.normal(value_sample, (SEQUENCE_TOKENS, KEY_VALUE_HEADS, HEAD_SIZE), jnp.float32), -5.0, 5.0)
    query_rows = jnp.clip(jax.random.normal(query_sample, (SEQUENCE_TOKENS, KEY_VALUE_HEADS, QUERY_PER_KV, HEAD_SIZE), jnp.float32), -5.0, 5.0)
    packed_pair = jnp.stack([key_rows.reshape(SEQUENCE_TOKENS, KEY_VALUE_HEADS * HEAD_SIZE), value_rows.reshape(SEQUENCE_TOKENS, KEY_VALUE_HEADS * HEAD_SIZE)], axis=0)
    return (query_rows.reshape(SEQUENCE_TOKENS, HQ * HEAD_SIZE), packed_pair)


def draw_queries(key, part):
    return activations(key)[0].astype(jnp.bfloat16)


def draw_key_value_pair(key, part):
    return activations(key)[1].astype(jnp.bfloat16)


def split_up(number_of, total, most, lean):
    weights = [(1 << 20) // math.isqrt(rank ** lean) + 1 for rank in range(2, number_of + 1)]
    spare, holding = total - most - (number_of - 1), [1] * (number_of - 1)
    while spare > 0:
        candidates = [i for i in range(number_of - 1) if holding[i] < most]
        whole, remaining = sum([weights[i] for i in candidates]), spare
        for i in candidates:
            extra = min(most - holding[i], max(1, remaining * weights[i] // whole), spare)
            holding[i] = holding[i] + extra
            spare = spare - extra
    return np.array([most] + holding)


def uneven(stream_key, count, total, most, skew):
    if count == 2:
        one = jax.random.randint(stream_key, (), max(1, total - most), min(most, total - 1) + 1)
        return jnp.stack([one, total - one])
    tallies = jnp.asarray(split_up(count, total, most, skew), jnp.int32)
    pairs = (count - 1) // 2
    source_of, receiver = tallies[1:1 + 2 * pairs:2], tallies[2:2 + 2 * pairs:2]
    slack = jnp.minimum(source_of - 1, most - receiver)
    moved = jax.random.randint(jax.random.fold_in(stream_key, 1), (pairs,), 0, 1 << 20) % (slack + 1)
    tallies = tallies.at[1:1 + 2 * pairs:2].set(source_of - moved).at[2:2 + 2 * pairs:2].set(receiver + moved)
    return tallies[jax.random.permutation(jax.random.fold_in(stream_key, 2), count)]


def setup_inputs(seed: int = 0) -> dict:
    key_list = jax.random.split(jax.random.key(seed), 4)
    return {
        "queries": draw_queries(jax.random.fold_in(key_list[3], 71), 0),
        "key_value_pair": draw_key_value_pair(jax.random.fold_in(key_list[3], 71), 0),
        "lengths": uneven(key_list[2], NDOC, SEQUENCE_TOKENS, LONGEST, 2).astype(jnp.int32),
    }


def doc_start(doc_lengths, row_ids):
    doc_ends = jnp.cumsum(doc_lengths).astype(jnp.int32)
    passed = doc_ends[None, :] <= row_ids[:, None]
    return jnp.max(jnp.where(passed, doc_ends[None, :], 0), axis=1).astype(jnp.int32)


def apply_rotary(vectors, positions):
    half_width = vectors.shape[-1] // 2
    steps_up = jnp.arange(half_width, dtype=jnp.float32) * (2.0 / vectors.shape[-1])
    inverse = jnp.exp(-steps_up * math.log(500000.0))
    angles = positions[:, None] * inverse[None, :]
    cosine = jnp.cos(angles)[:, None, :]
    sine_table = jnp.sin(angles)[:, None, :]
    low_half = vectors[..., :half_width]
    high_half = vectors[..., half_width:]
    return jnp.concatenate([low_half * cosine - high_half * sine_table, high_half * cosine + low_half * sine_table], axis=-1)


def reference(queries, key_value_pair, lengths):
    score_scale = HEAD_SIZE ** -0.5
    row_ids = jnp.arange(SEQUENCE_TOKENS, dtype=jnp.int32)
    starts = doc_start(lengths, row_ids)
    positions = (row_ids - starts).astype(jnp.float32)
    query_rotated = apply_rotary(queries.reshape(SEQUENCE_TOKENS, HQ, HEAD_SIZE).astype(jnp.float32), positions).astype(jnp.bfloat16)
    key_rotated = apply_rotary(key_value_pair[0].reshape(SEQUENCE_TOKENS, KEY_VALUE_HEADS, HEAD_SIZE).astype(jnp.float32), positions).astype(jnp.bfloat16)
    value_rows = key_value_pair[1].reshape(SEQUENCE_TOKENS, KEY_VALUE_HEADS, HEAD_SIZE)
    query_heads = jnp.transpose(query_rotated.reshape(SEQUENCE_TOKENS, KEY_VALUE_HEADS, QUERY_PER_KV, HEAD_SIZE), (1, 0, 2, 3))
    key_heads = jnp.transpose(key_rotated, (1, 0, 2))
    value_heads = jnp.transpose(value_rows, (1, 0, 2))
    pieces = []
    for owner_index in range(N_SRV):
        row_low = owner_index * TOK_DEV
        row_high = row_low + TOK_DEV
        shard_count = owner_index + 1
        own_rows = row_ids[row_low:row_high]
        own_starts = starts[row_low:row_high]
        key_ids = jnp.arange(row_high, dtype=jnp.int32).reshape(shard_count, TOK_DEV)
        allowed = (key_ids[None] <= own_rows[:, None, None]) & (key_ids[None] >= own_starts[:, None, None])

        def one_head(packed, allowed=allowed, shard_count=shard_count):
            head_query, head_key, head_value = packed
            scores = jnp.einsum('rgd,ckd->grck', head_query.astype(jnp.float32),
                                head_key.reshape(shard_count, TOK_DEV, HEAD_SIZE).astype(jnp.float32)) * score_scale
            masked = jnp.where(allowed[None], scores, -1e30)
            shard_max = jnp.max(masked, axis=3)
            weights = jnp.where(allowed[None], jnp.exp(masked - shard_max[..., None]), 0.0)
            shard_total = jnp.sum(weights, axis=3)
            rounded = lax.optimization_barrier(weights.astype(jnp.bfloat16)).astype(jnp.float32)
            part_value = jnp.einsum('grck,ckd->grcd', rounded,
                                    head_value.reshape(shard_count, TOK_DEV, HEAD_SIZE).astype(jnp.float32))
            top_max = jnp.max(shard_max, axis=2)
            share = jnp.exp(shard_max - top_max[..., None])
            summed = jnp.sum(share[..., None] * part_value, axis=2)
            row_total = jnp.sum(share * shard_total, axis=2)
            return summed / row_total[..., None]

        per_head = lax.map(one_head, (query_heads[:, row_low:row_high], key_heads[:, :row_high], value_heads[:, :row_high]))
        pieces.append(jnp.transpose(per_head, (2, 0, 1, 3)).reshape(TOK_DEV, HQ * HEAD_SIZE))
    return jnp.concatenate(pieces, axis=0).astype(jnp.bfloat16)
```

```python
import functools
import math

import jax
import jax.numpy as jnp
from jax import lax
from jax.experimental import pallas as pl
from jax.experimental.pallas import tpu as pltpu
from jax.sharding import PartitionSpec as P

HEAD = 128
MESH = pl.DeviceIdType.MESH


def kernel(cfg, len_ref, q_ref, kv_ref, out_ref, qraw, qrot, kvbuf, kvin, ksend, fkv, table, bias,
           sc0, mx0, obuf, lsem, qs, qr, kvs, kvr, fwd, xs, xr, fs, fr, hs, osend, orecv):
    n_srv, n_head, G, back, tok, kvh, per, R, chunk, ndoc, swap = cfg
    heads = kvh * per
    grp = G * tok
    n_grp = n_srv // G
    T = tok // n_head
    longest = back * grp
    W = longest + R
    width = heads * HEAD
    kw = kvh * HEAD
    nbm = tok // R
    nblk = grp // R
    nch = heads // chunk
    units = nblk * nch
    per_blk = R // T
    cw = chunk * HEAD
    rows_u = chunk * R
    srv = lax.axis_index("srv")
    z = lax.axis_index("head")
    k = srv // G
    a = srv % G

    mine_half = z // (n_head // nbm)
    partner = n_head - 1 - z
    if swap:
        inner = jnp.logical_or(z == n_head // 2 - 1, z == n_head // 2)
    else:
        inner = z < 0
    swapped = jnp.logical_and(inner, a == G - 1)

    bar = pltpu.get_barrier_semaphore()

    def greet(s, h):
        pl.semaphore_signal(bar, inc=1, device_id=(s, h), device_id_type=MESH)

    for i in range(1, n_head):
        for b in range(G):
            greet(k * G + b, (z + i) % n_head)
    for i in range(1, G):
        greet(k * G + (a + i) % G, z)
    for d in range(1, back + 1):
        @pl.when(k + d < n_grp)
        def _():
            for b in range(G):
                greet((k + d) * G + b, z)

        @pl.when(k - d >= 0)
        def _():
            for b in range(G):
                greet((k - d) * G + b, z)

    own_kv = pltpu.make_async_copy(kv_ref, kvin, lsem.at[0])
    own_kv.start()

    def cols_of(b):
        return pl.ds(pl.multiple_of(b * width, HEAD), width)

    def part_rows(p):
        return slice(p * R, (p + 1) * R)

    def own_q(p):
        return pltpu.make_async_copy(q_ref.at[part_rows(p), cols_of(a)], qraw.at[a, p], qr.at[a, p])

    def kept(p):
        return jnp.logical_not(jnp.logical_and(swapped, mine_half != p))

    for p in range(nbm):
        @pl.when(kept(p))
        def _():
            own_q(p).start()

    ends = []
    total = jnp.int32(0)
    for i in range(ndoc):
        total = total + len_ref[i]
        ends.append(total)

    lane = lax.broadcasted_iota(jnp.int32, (tok, HEAD), 1)
    low = lane < HEAD // 2
    step_up = jnp.where(low, lane, lane - HEAD // 2).astype(jnp.float32) * (2.0 / HEAD)
    inverse = jnp.exp(-step_up * math.log(500000.0))

    def starts_of(rows):
        start = jnp.zeros_like(rows)
        for e in ends:
            start = jnp.where(e <= rows, e, start)
        return start

    def cos_sin(angle):
        turns = jnp.floor(angle * (2.0 / math.pi) + 0.5)
        r = ((angle - turns * 1.5703125) - turns * 4.837512969970703125e-4) - turns * 7.549789948768648e-8
        r2 = r * r
        s = r + r * r2 * (-1.6666654611e-1 + r2 * (8.3321608736e-3 - r2 * 1.9515295891e-4))
        c = 1.0 - 0.5 * r2 + r2 * r2 * (
            4.166664568298827e-2 + r2 * (-1.388731625493765e-3 + r2 * 2.443315711809948e-5))
        quarter = turns.astype(jnp.int32)
        odd = (quarter & 1) == 1
        sine = jnp.where(odd, c, s)
        cosine = jnp.where(odd, s, c)
        sine = jnp.where((quarter & 2) == 2, -sine, sine)
        cosine = jnp.where(((quarter + 1) & 2) == 2, -cosine, cosine)
        return cosine, sine

    def make_table(b):
        rows = (k * G + b) * tok + lax.broadcasted_iota(jnp.int32, (tok, HEAD), 0)
        angle = (rows - starts_of(rows)).astype(jnp.float32) * inverse
        cosine, sine = cos_sin(angle)
        table[b, 0] = cosine
        table[b, 1] = jnp.where(low, -sine, sine)

    def rotate(x, cosine, sine):
        x = x.astype(jnp.float32)
        return (x * cosine + pltpu.roll(x, HEAD // 2, 1) * sine).astype(jnp.bfloat16)

    make_table(a)
    own_kv.wait()
    for h in range(G * kvh):
        cols = slice(h * HEAD, (h + 1) * HEAD)
        ksend[:, cols] = rotate(kvin[0, :, cols], table[a, 0], table[a, 1])

    own_rows = pl.ds(pl.multiple_of(back * grp + a * tok, tok), tok)
    kv_cols = pl.ds(pl.multiple_of(a * kw, HEAD), kw)
    kvbuf[0, 0, own_rows, :] = ksend[:, kv_cols]
    kvbuf[0, 1, own_rows, :] = kvin[1, :, kv_cols]

    count = (n_head - 1) * G + (G - 1)
    for d in range(1, back + 1):
        count = count + G * jnp.where(k + d < n_grp, 1, 0) + G * jnp.where(k - d >= 0, 1, 0)
    pl.semaphore_wait(bar, count)

    def kv_copy(d, i, which):
        b = (a + i) % G
        cols = pl.ds(pl.multiple_of(b * kw, HEAD), kw)
        src = ksend.at[:, cols] if which == 0 else kvin.at[1, :, cols]
        rows = pl.ds(pl.multiple_of((back - d) * grp + a * tok, tok), tok)
        return pltpu.make_async_remote_copy(
            src_ref=src, dst_ref=kvbuf.at[0, which, rows, :],
            send_sem=kvs.at[d, i, which], recv_sem=kvr.at[d, a, which],
            device_id=((k + d) * G + b, z), device_id_type=MESH)

    def kv_wait(d, b, which):
        rows = pl.ds(pl.multiple_of((back - d) * grp + b * tok, tok), tok)
        ref = kvbuf.at[0, which, rows, :]
        pltpu.make_async_copy(ref, ref, kvr.at[d, b, which]).wait()

    odd_near = jnp.logical_and(k % 2 == 1, k + 2 < n_grp)
    relayed = jnp.logical_and(odd_near, a == G - 1)
    relays = jnp.logical_and(k % 2 == 1, k >= 3)

    def sends(d):
        near = k + d < n_grp
        if d == 1 and back >= 2:
            near = jnp.logical_and(near, jnp.logical_not(relayed))
        return near

    def relay_copy(b, which):
        src = pl.ds(pl.multiple_of((back - 2) * grp + b * tok, tok), tok)
        dst = pl.ds(pl.multiple_of((back - 1) * grp + b * tok, tok), tok)
        return pltpu.make_async_remote_copy(
            src_ref=kvbuf.at[0, which, src, :], dst_ref=kvbuf.at[0, which, dst, :],
            send_sem=fwd.at[b, which], recv_sem=kvr.at[1, b, which],
            device_id=(srv - G, z), device_id_type=MESH)

    def start_kv(d, when):
        @pl.when(jnp.logical_and(sends(d), when))
        def _():
            pairs = [(i, which) for which in range(2) for i in range(G)]
            for i, which in pairs if d == 1 else sorted(pairs):
                kv_copy(d, i, which).start()

    moved = pl.ds((G - 1) * kw, kw)

    def cross_kv(which):
        src = ksend.at[:, moved] if which == 0 else kvin.at[1, :, moved]
        return pltpu.make_async_remote_copy(
            src_ref=src, dst_ref=fkv.at[which], send_sem=xs.at[which], recv_sem=xr.at[which],
            device_id=(srv, partner), device_id_type=MESH)

    def cross_q():
        there = nbm - 1 - mine_half
        src = pl.ds(pl.multiple_of(there * R, R), R)
        return pltpu.make_async_remote_copy(
            src_ref=q_ref.at[src, pl.ds((G - 1) * width, width)], dst_ref=qraw.at[a, mine_half],
            send_sem=xs.at[2], recv_sem=qr.at[a, mine_half],
            device_id=(k * G + G - 1, partner), device_id_type=MESH)

    def chip_q(i, p):
        b = (a + i) % G
        return pltpu.make_async_remote_copy(
            src_ref=q_ref.at[part_rows(p), cols_of(b)], dst_ref=qraw.at[a, p],
            send_sem=qs.at[i, p], recv_sem=qr.at[a, p],
            device_id=(k * G + b, z), device_id_type=MESH)

    def chip_kept(i, p):
        b = (a + i) % G
        away = jnp.logical_and(jnp.logical_and(inner, b == G - 1), mine_half != p)
        return jnp.logical_not(away)

    for d in range(1, back + 1):
        start_kv(d, a == G - 1 if d == back else True)
    if swap:
        @pl.when(inner)
        def _():
            cross_kv(0).start()
            cross_kv(1).start()
            cross_q().start()
    for i in range(1, G):
        for which in range(2):
            kv_copy(0, i, which).start()
        for p in range(nbm):
            @pl.when(chip_kept(i, p))
            def _():
                chip_q(i, p).start()

    def q_wait(b, p):
        pltpu.make_async_copy(qraw.at[b, p], qraw.at[b, p], qr.at[b, p]).wait()

    def rotate_queries(b, p, part):
        rows = pl.ds(pl.multiple_of(part * R, R), R)
        cosine = table[b, 0, rows, :]
        sine = table[b, 1, rows, :]
        dst = pl.ds(pl.multiple_of((b * nbm + p) * R, R), R)
        for h in range(heads):
            qrot[h, dst, :] = rotate(qraw[b, p, :, h * HEAD:(h + 1) * HEAD], cosine, sine)

    def take_queries(b):
        for p in range(nbm):
            @pl.when(kept(p))
            def _():
                q_wait(b, p)
                rotate_queries(b, p, p)

    for d in range(1, back + 1):
        @pl.when(k - d < 0)
        def _():
            for sel in range(2 if swap else 1):
                kvbuf[sel, :, pl.ds((back - d) * grp, grp), :] = jnp.zeros((2, grp, kw), jnp.bfloat16)

    take_queries(a)
    start_kv(back, a < G - 1)
    for i in range(1, G):
        b = (a + i) % G
        make_table(b)
        take_queries(b)

    def pass_copy(d, which):
        rows = pl.ds(pl.multiple_of((back - d) * grp + a * tok, tok), tok)
        return pltpu.make_async_remote_copy(
            src_ref=fkv.at[which], dst_ref=kvbuf.at[1, which, rows, :],
            send_sem=fs.at[d, which], recv_sem=fr.at[d, a, which],
            device_id=((k + d) * G + G - 1, z), device_id_type=MESH)

    def passes(d):
        if d == 0:
            return a < G - 1
        near = k + d < n_grp
        if d == 1 and back >= 2:
            near = jnp.logical_and(near, jnp.logical_not(odd_near))
        return near

    hands_on = jnp.logical_and(relays, swapped)

    def hand_copy(b, which):
        src = pl.ds(pl.multiple_of((back - 2) * grp + b * tok, tok), tok)
        dst = pl.ds(pl.multiple_of((back - 1) * grp + b * tok, tok), tok)
        return pltpu.make_async_remote_copy(
            src_ref=kvbuf.at[1, which, src, :], dst_ref=kvbuf.at[1, which, dst, :],
            send_sem=hs.at[b, which], recv_sem=fr.at[1, b, which],
            device_id=(srv - G, z), device_id_type=MESH)

    def moved_wait(d, b, which):
        rows = pl.ds((back - d) * grp + b * tok, tok)
        ref = kvbuf.at[1, which, rows, :]
        pltpu.make_async_copy(ref, ref, fr.at[d, b, which]).wait()

    def pass_on(which):
        @pl.when(inner)
        def _():
            pltpu.make_async_copy(fkv.at[which], fkv.at[which], xr.at[which]).wait()
            for d in range(back, -1, -1):
                @pl.when(passes(d))
                def _():
                    pass_copy(d, which).start()

            @pl.when(swapped)
            def _():
                kvbuf[1, which, own_rows, :] = fkv[which]

    for which in range(2):
        if back >= 2:
            @pl.when(relays)
            def _():
                kv_wait(2, G - 1, which)
                relay_copy(G - 1, which).start()
        if swap:
            pass_on(which)

    def wait_moved():
        for which in range(2):
            for d in range(back + 1):
                for b in range(G):
                    if d == 0:
                        if b < G - 1:
                            moved_wait(d, b, which)
                    else:
                        ready = k - d >= 0
                        if d == 2:
                            ready = jnp.logical_and(ready, jnp.logical_not(relays))

                        @pl.when(ready)
                        def _():
                            moved_wait(d, b, which)

    def kv_wait_new(d, b, which):
        if (d, b) == (2, G - 1):
            @pl.when(jnp.logical_not(relays))
            def _():
                kv_wait(d, b, which)
        else:
            kv_wait(d, b, which)

    def wait_early(which):
        for i in range(1, G):
            kv_wait(0, (a + i) % G, which)
        for d in range(1, back + 1):
            @pl.when(k - d >= 0)
            def _():
                for b in range(G - 1 if d == back else 0, G):
                    kv_wait_new(d, b, which)

    def wait_late():
        @pl.when(k - back >= 0)
        def _():
            for b in range(G - 1):
                for which in range(2):
                    kv_wait_new(back, b, which)

    wait_early(0)

    edge = n_head // 4
    outer = jnp.logical_or(z < edge, z >= n_head - edge)
    scale = HEAD ** -0.5 * math.log2(math.e)

    def where_of(u):
        blk = u // nch
        c = u % nch
        late = jnp.where(blk == 0, 0, jnp.where(blk == nblk - 1, 1, blk + 1))
        blk = jnp.where(outer, late, blk)
        b = G - 1 - blk % G
        slot = (mine_half + jnp.where(swapped, 0, 1) + blk // G) % nbm
        foreign = jnp.where(jnp.logical_and(swapped, slot != mine_half), 1, 0)
        part = jnp.where(foreign == 1, mine_half, slot)
        return c, b, slot, part, foreign

    def make_bias(u):
        c, b, slot, part, foreign = where_of(u)
        r0 = pl.multiple_of(b * tok + part * R, R)
        rows = k * grp + r0 + lax.broadcasted_iota(jnp.int32, (R, HEAD), 0)
        start = starts_of(rows)
        for j in range(W // HEAD):
            t = (k - back) * grp + r0 + j * HEAD + lax.broadcasted_iota(jnp.int32, (R, HEAD), 1)
            ok = jnp.logical_and(t >= start, t <= rows)
            bias[:, j * HEAD:(j + 1) * HEAD] = jnp.where(ok, 0.0, -1e30)

    def scores(u, sc, mx):
        c, b, slot, part, foreign = where_of(u)
        r0 = pl.multiple_of(b * tok + part * R, R)
        q0 = pl.multiple_of((b * nbm + slot) * R, R)
        kcol = pl.ds(pl.multiple_of((c * chunk // per) * HEAD, HEAD), HEAD)
        q = qrot[pl.ds(c * chunk, chunk), pl.ds(q0, R), :].reshape(rows_u, HEAD)
        top = None
        for t0 in range(0, W, 2 * HEAD):
            n = min(2 * HEAD, W - t0)
            keys = kvbuf[foreign, 0, pl.ds(pl.multiple_of(r0 + t0, HEAD), n), kcol]
            s = lax.dot_general(q, keys, (((1,), (1,)), ((), ())), preferred_element_type=jnp.float32)
            s = (s.reshape(chunk, R, n) + bias[:, t0:t0 + n][None]).reshape(rows_u, n)
            sc[:, t0:t0 + n] = s
            m = functools.reduce(jnp.maximum, [s[:, h:h + HEAD] for h in range(0, n, HEAD)])
            top = m if top is None else jnp.maximum(top, m)
        mx[...] = jnp.broadcast_to(jnp.max(top, axis=1, keepdims=True), (rows_u, HEAD))

    def attend(u, sc, mx):
        c, b, slot, part, foreign = where_of(u)
        r0 = pl.multiple_of(b * tok + part * R, R)
        kcol = pl.ds(pl.multiple_of((c * chunk // per) * HEAD, HEAD), HEAD)
        top = mx[...]
        acc = None
        for t0 in range(0, W, 2 * HEAD):
            n = min(2 * HEAD, W - t0)
            peak = jnp.concatenate([top] * (n // HEAD), axis=1)
            w = jnp.exp2((sc[:, t0:t0 + n] - peak) * scale).astype(jnp.bfloat16)
            vals = kvbuf[foreign, 1, pl.ds(pl.multiple_of(r0 + t0, HEAD), n), kcol]
            vals = jnp.concatenate([vals, jnp.ones_like(vals)], axis=1)
            part_acc = lax.dot_general(w, vals, (((1,), (0,)), ((), ())), preferred_element_type=jnp.float32)
            acc = part_acc if acc is None else acc + part_acc
        o = (acc[:, :HEAD] / acc[:, HEAD:]).astype(jnp.bfloat16)
        for h in range(chunk):
            obuf[u, :, h * HEAD:(h + 1) * HEAD] = o[h * R:(h + 1) * R, :]

    def out_copy(u, j):
        c, b, slot, part, foreign = where_of(u)
        dest = part * per_blk + j
        zsrc = jnp.where(foreign == 1, partner, z)
        col = pl.multiple_of(zsrc * (G * width) + a * width + c * cw, HEAD)
        src = obuf.at[u, pl.ds(j * T, T), :]
        dst = out_ref.at[:, pl.ds(col, cw)]
        idx = (zsrc * G + a) * nch + c
        remote = pltpu.make_async_remote_copy(
            src_ref=src, dst_ref=dst, send_sem=osend.at[u * per_blk + j], recv_sem=orecv.at[idx],
            device_id=(k * G + b, dest), device_id_type=MESH)
        local = pltpu.make_async_copy(src, dst, orecv.at[idx])
        mine = jnp.logical_and(b == a, dest == z)
        return mine, remote, local

    def send_out(u):
        for j in range(per_blk):
            mine, remote, local = out_copy(u, j)

            @pl.when(mine)
            def _():
                local.start()

            @pl.when(jnp.logical_not(mine))
            def _():
                remote.start()

    def open_block(u):
        blk = u // nch

        @pl.when(blk == 1)
        def _():
            wait_late()

        if swap and back >= 2:
            @pl.when(jnp.logical_and(hands_on, blk == 1))
            def _():
                for which in range(2):
                    for b in range(G):
                        moved_wait(2, b, which)
                        hand_copy(b, which).start()

        if swap:
            @pl.when(jnp.logical_and(swapped, blk == nblk // nbm))
            def _():
                wait_moved()
                for b in range(G):
                    q_wait(b, nbm - 1 - mine_half)
                    rotate_queries(b, nbm - 1 - mine_half, mine_half)

        make_bias(u)

    make_bias(0)
    scores(0, sc0, mx0)
    wait_early(1)

    def one_step(u, carry):
        @pl.when(jnp.logical_and((u + 1) % nch == 0, u + 1 < units))
        def _():
            open_block(u + 1)

        attend(u, sc0, mx0)
        scores(jnp.minimum(u + 1, units - 1), sc0, mx0)
        send_out(u)
        return carry

    lax.fori_loop(0, units, one_step, 0)

    for i in range(1, G):
        for which in (1, 0):
            kv_copy(0, i, which).wait_send()
        for p in range(nbm):
            @pl.when(chip_kept(i, p))
            def _():
                chip_q(i, p).wait_send()
    for d in range(1, back + 1):
        @pl.when(sends(d))
        def _():
            for i in range(G):
                for which in (1, 0):
                    kv_copy(d, i, which).wait_send()
    if back >= 2:
        @pl.when(relays)
        def _():
            for which in range(2):
                relay_copy(G - 1, which).wait_send()
    if swap:
        @pl.when(inner)
        def _():
            if back >= 2:
                @pl.when(hands_on)
                def _():
                    for which in range(2):
                        for b in range(G):
                            hand_copy(b, which).wait_send()

            cross_q().wait_send()
            for which in range(2):
                cross_kv(which).wait_send()
                for d in range(back + 1):
                    @pl.when(passes(d))
                    def _():
                        pass_copy(d, which).wait_send()

    def end_send(u, carry):
        for j in range(per_blk):
            mine, remote, local = out_copy(u, j)

            @pl.when(jnp.logical_not(mine))
            def _():
                remote.wait_send()
        return carry

    lax.fori_loop(0, units, end_send, 0)

    def end_recv(i, carry):
        col = pl.multiple_of(i * cw, HEAD)
        ref = out_ref.at[:, pl.ds(col, cw)]
        pltpu.make_async_copy(ref, ref, orecv.at[i]).wait()
        return carry

    lax.fori_loop(0, n_head * G * nch, end_recv, 0)


def solution(mesh):
    n_srv, n_head = mesh.shape["srv"], mesh.shape["head"]

    def body(queries, key_value_pair, lengths):
        tok, qw = queries.shape
        kv_all = key_value_pair.shape[2] // HEAD
        G = 2 if kv_all % 2 == 0 and n_srv % 2 == 0 else 1
        kvh = kv_all // G
        per = qw // HEAD // kv_all
        grp = G * tok
        n_grp = n_srv // G
        back = n_grp // 2
        T = tok // n_head
        R = max(tok // 2, T)
        chunk = per // 4
        ndoc = lengths.shape[0]
        heads = kvh * per
        nch = heads // chunk
        units = (grp // R) * nch
        W = back * grp + R
        swap = True and G == 2 and n_head % 2 == 0 and tok // R == 2
        cfg = (n_srv, n_head, G, back, tok, kvh, per, R, chunk, ndoc, swap)
        bf = jnp.bfloat16
        dma = pltpu.SemaphoreType.DMA
        return pl.pallas_call(
            functools.partial(kernel, cfg),
            out_shape=pltpu.VMEM((T, qw * n_head), bf),
            in_specs=[
                pl.BlockSpec(memory_space=pltpu.SMEM),
                pl.BlockSpec(memory_space=pl.ANY),
                pl.BlockSpec(memory_space=pl.ANY),
            ],
            out_specs=pl.BlockSpec(memory_space=pl.ANY),
            scratch_shapes=[
                pltpu.VMEM((G, tok // R, R, heads * HEAD), bf),
                pltpu.VMEM((heads, grp, HEAD), bf),
                pltpu.VMEM((2, 2, (back + 1) * grp, kvh * HEAD), bf),
                pltpu.VMEM((2, tok, kv_all * HEAD), bf),
                pltpu.VMEM((tok, kv_all * HEAD), bf),
                pltpu.VMEM((2, tok, kvh * HEAD), bf),
                pltpu.VMEM((G, 2, tok, HEAD), jnp.float32),
                pltpu.VMEM((R, W), jnp.float32),
                pltpu.VMEM((chunk * R, W), jnp.float32),
                pltpu.VMEM((chunk * R, HEAD), jnp.float32),
                pltpu.VMEM((units, R, chunk * HEAD), bf),
                dma((1,)),
                dma((G, tok // R)),
                dma((G, tok // R)),
                dma((back + 1, G, 2)),
                dma((back + 1, G, 2)),
                dma((G, 2)),
                dma((3,)),
                dma((2,)),
                dma((back + 1, 2)),
                dma((back + 1, G, 2)),
                dma((G, 2)),
                dma((units * (R // T),)),
                dma((n_head * G * nch,)),
            ],
            compiler_params=pltpu.CompilerParams(collective_id=0, has_side_effects=True),
            name="attend",
        )(lengths, queries, key_value_pair)

    in_specs = (P("srv", "head"), P(None, "srv", "head"), P())
    out_specs = P(("srv", "head"), None)
    return jax.shard_map(body, mesh=mesh, in_specs=in_specs, out_specs=out_specs, check_vma=False)
```

```python
import functools
import math

import jax
import jax.numpy as jnp
from jax import lax
from jax.experimental import pallas as pl
from jax.experimental.pallas import tpu as pltpu
from jax.sharding import PartitionSpec as P

HEAD = 128
ORDS = ((0, 2, 3, 1), (2, 0, 1, 3), (0, 2, 3, 1), (0, 2, 3, 1), (2, 3, 0, 1), (0, 2, 3, 1))
MESH = pl.DeviceIdType.MESH


def kernel(cfg, len_ref, q_ref, kv_ref, out_ref, qraw, qrot, kvbuf, kvin, ksend, fkv, table, bias,
           sc0, mx0, obuf, lsem, qs, qr, kvs, kvr, fwd, xs, xr, fs, fr, hs, osend, orecv):
    n_srv, n_head, G, back, tok, kvh, per, R, chunk, ndoc, swap = cfg
    heads = kvh * per
    grp = G * tok
    n_grp = n_srv // G
    T = tok // n_head
    longest = back * grp
    W = longest + R
    width = heads * HEAD
    kw = kvh * HEAD
    nbm = tok // R
    nblk = grp // R
    nch = heads // chunk
    units = nblk * nch
    per_blk = R // T
    cw = chunk * HEAD
    rows_u = chunk * R
    srv = lax.axis_index("srv")
    z = lax.axis_index("head")
    k = srv // G
    a = srv % G

    mine_half = z // (n_head // nbm)
    partner = n_head - 1 - z
    if swap:
        inner = jnp.logical_or(z == n_head // 2 - 1, z == n_head // 2)
    else:
        inner = z < 0
    serves = inner
    swapped = jnp.logical_and(serves, a == G - 1)

    bar = pltpu.get_barrier_semaphore()

    def greet(s, h):
        pl.semaphore_signal(bar, inc=1, device_id=(s, h), device_id_type=MESH)

    for i in range(1, n_head):
        for b in range(G):
            greet(k * G + b, (z + i) % n_head)
    for i in range(1, G):
        greet(k * G + (a + i) % G, z)
    for d in range(1, back + 1):
        @pl.when(k + d < n_grp)
        def _():
            for b in range(G):
                greet((k + d) * G + b, z)

        @pl.when(k - d >= 0)
        def _():
            for b in range(G):
                greet((k - d) * G + b, z)

    own_kv = pltpu.make_async_copy(kv_ref, kvin, lsem.at[0])
    own_kv.start()

    def cols_of(b):
        return pl.ds(pl.multiple_of(b * width, HEAD), width)

    def part_rows(p):
        return slice(p * R, (p + 1) * R)

    def own_q(p):
        return pltpu.make_async_copy(q_ref.at[part_rows(p), cols_of(a)], qraw.at[a, p], qr.at[a, p])

    def kept(p):
        return jnp.logical_not(jnp.logical_and(swapped, mine_half != p))

    for p in range(nbm):
        @pl.when(kept(p))
        def _():
            own_q(p).start()

    ends = []
    total = jnp.int32(0)
    for i in range(ndoc):
        total = total + len_ref[i]
        ends.append(total)

    lane = lax.broadcasted_iota(jnp.int32, (tok, HEAD), 1)
    low = lane < HEAD // 2
    step_up = jnp.where(low, lane, lane - HEAD // 2).astype(jnp.float32) * (2.0 / HEAD)
    inverse = jnp.exp(-step_up * math.log(500000.0))

    def starts_of(rows):
        start = jnp.zeros_like(rows)
        for e in ends:
            start = jnp.where(e <= rows, e, start)
        return start

    def cos_sin(angle):
        turns = jnp.floor(angle * (2.0 / math.pi) + 0.5)
        r = ((angle - turns * 1.5703125) - turns * 4.837512969970703125e-4) - turns * 7.549789948768648e-8
        r2 = r * r
        s = r + r * r2 * (-1.6666654611e-1 + r2 * (8.3321608736e-3 - r2 * 1.9515295891e-4))
        c = 1.0 - 0.5 * r2 + r2 * r2 * (
            4.166664568298827e-2 + r2 * (-1.388731625493765e-3 + r2 * 2.443315711809948e-5))
        quarter = turns.astype(jnp.int32)
        odd = (quarter & 1) == 1
        sine = jnp.where(odd, c, s)
        cosine = jnp.where(odd, s, c)
        sine = jnp.where((quarter & 2) == 2, -sine, sine)
        cosine = jnp.where(((quarter + 1) & 2) == 2, -cosine, cosine)
        return cosine, sine

    def make_table(b):
        rows = (k * G + b) * tok + lax.broadcasted_iota(jnp.int32, (tok, HEAD), 0)
        angle = (rows - starts_of(rows)).astype(jnp.float32) * inverse
        cosine, sine = cos_sin(angle)
        table[b, 0] = cosine
        table[b, 1] = jnp.where(low, -sine, sine)

    def rotate(x, cosine, sine):
        x = x.astype(jnp.float32)
        return (x * cosine + pltpu.roll(x, HEAD // 2, 1) * sine).astype(jnp.bfloat16)

    make_table(a)
    own_kv.wait()
    for h in range(G * kvh):
        cols = slice(h * HEAD, (h + 1) * HEAD)
        ksend[:, cols] = rotate(kvin[0, :, cols], table[a, 0], table[a, 1])

    own_rows = pl.ds(pl.multiple_of(back * grp + a * tok, tok), tok)
    kv_cols = pl.ds(pl.multiple_of(a * kw, HEAD), kw)
    kvbuf[0, 0, own_rows, :] = ksend[:, kv_cols]
    kvbuf[0, 1, own_rows, :] = kvin[1, :, kv_cols]

    count = (n_head - 1) * G + (G - 1)
    for d in range(1, back + 1):
        count = count + G * jnp.where(k + d < n_grp, 1, 0) + G * jnp.where(k - d >= 0, 1, 0)
    pl.semaphore_wait(bar, count)

    def kv_copy(d, i, which):
        b = (a + i) % G
        cols = pl.ds(pl.multiple_of(b * kw, HEAD), kw)
        src = ksend.at[:, cols] if which == 0 else kvin.at[1, :, cols]
        rows = pl.ds(pl.multiple_of((back - d) * grp + a * tok, tok), tok)
        return pltpu.make_async_remote_copy(
            src_ref=src, dst_ref=kvbuf.at[0, which, rows, :],
            send_sem=kvs.at[d, i, which], recv_sem=kvr.at[d, a, which],
            device_id=((k + d) * G + b, z), device_id_type=MESH)

    def kv_wait(d, b, which):
        rows = pl.ds(pl.multiple_of((back - d) * grp + b * tok, tok), tok)
        ref = kvbuf.at[0, which, rows, :]
        pltpu.make_async_copy(ref, ref, kvr.at[d, b, which]).wait()

    odd_near = jnp.logical_and(k % 2 == 1, k + 2 < n_grp)
    relayed = jnp.logical_and(odd_near, a == G - 1)
    relays = jnp.logical_and(k % 2 == 1, k >= 3)

    def sends(d):
        near = k + d < n_grp
        if d == 1 and back >= 2:
            near = jnp.logical_and(near, jnp.logical_not(relayed))
        return near

    def relay_copy(b, which):
        src = pl.ds(pl.multiple_of((back - 2) * grp + b * tok, tok), tok)
        dst = pl.ds(pl.multiple_of((back - 1) * grp + b * tok, tok), tok)
        return pltpu.make_async_remote_copy(
            src_ref=kvbuf.at[0, which, src, :], dst_ref=kvbuf.at[0, which, dst, :],
            send_sem=fwd.at[b, which], recv_sem=kvr.at[1, b, which],
            device_id=(srv - G, z), device_id_type=MESH)

    def start_kv(d, when):
        @pl.when(jnp.logical_and(sends(d), when))
        def _():
            pairs = [(i, which) for which in range(2) for i in range(G)]
            for i, which in pairs if d == 1 else sorted(pairs):
                kv_copy(d, i, which).start()

    moved = pl.ds((G - 1) * kw, kw)

    def cross_kv(which):
        src = ksend.at[:, moved] if which == 0 else kvin.at[1, :, moved]
        return pltpu.make_async_remote_copy(
            src_ref=src, dst_ref=fkv.at[which], send_sem=xs.at[which], recv_sem=xr.at[which],
            device_id=(srv, partner), device_id_type=MESH)

    def cross_q():
        there = nbm - 1 - mine_half
        src = pl.ds(pl.multiple_of(there * R, R), R)
        return pltpu.make_async_remote_copy(
            src_ref=q_ref.at[src, pl.ds((G - 1) * width, width)], dst_ref=qraw.at[a, mine_half],
            send_sem=xs.at[2], recv_sem=qr.at[a, mine_half],
            device_id=(k * G + G - 1, partner), device_id_type=MESH)

    def chip_q(i, p):
        b = (a + i) % G
        return pltpu.make_async_remote_copy(
            src_ref=q_ref.at[part_rows(p), cols_of(b)], dst_ref=qraw.at[a, p],
            send_sem=qs.at[i, p], recv_sem=qr.at[a, p],
            device_id=(k * G + b, z), device_id_type=MESH)

    def chip_kept(i, p):
        b = (a + i) % G
        away = jnp.logical_and(jnp.logical_and(serves, b == G - 1), mine_half != p)
        return jnp.logical_not(away)

    if swap:
        @pl.when(inner)
        def _():
            cross_kv(0).start()
            cross_kv(1).start()
    for d in range(1, back + 1):
        start_kv(d, a == G - 1 if d == back else True)
    if swap:
        @pl.when(serves)
        def _():
            cross_q().start()
    for i in range(1, G):
        for which in range(2):
            kv_copy(0, i, which).start()
        for p in range(nbm):
            @pl.when(chip_kept(i, p))
            def _():
                chip_q(i, p).start()

    def q_wait(b, p):
        pltpu.make_async_copy(qraw.at[b, p], qraw.at[b, p], qr.at[b, p]).wait()

    def rotate_queries(b, p, part):
        rows = pl.ds(pl.multiple_of(part * R, R), R)
        cosine = table[b, 0, rows, :]
        sine = table[b, 1, rows, :]
        dst = pl.ds(pl.multiple_of((b * nbm + p) * R, R), R)
        for h in range(heads):
            qrot[h, dst, :] = rotate(qraw[b, p, :, h * HEAD:(h + 1) * HEAD], cosine, sine)

    def take_queries(b):
        for p in range(nbm):
            @pl.when(kept(p))
            def _():
                q_wait(b, p)
                rotate_queries(b, p, p)

    for d in range(1, back + 1):
        @pl.when(k - d < 0)
        def _():
            for sel in range(2 if swap else 1):
                kvbuf[sel, :, pl.ds((back - d) * grp, grp), :] = jnp.zeros((2, grp, kw), jnp.bfloat16)

    take_queries(a)
    for i in range(1, G):
        b = (a + i) % G
        make_table(b)
        take_queries(b)

    start_kv(back, a < G - 1)
    def pass_copy(d, which):
        rows = pl.ds(pl.multiple_of((back - d) * grp + a * tok, tok), tok)
        return pltpu.make_async_remote_copy(
            src_ref=fkv.at[which], dst_ref=kvbuf.at[1, which, rows, :],
            send_sem=fs.at[d, which], recv_sem=fr.at[d, a, which],
            device_id=((k + d) * G + G - 1, z), device_id_type=MESH)

    def passes(d):
        if d == 0:
            return a < G - 1
        near = k + d < n_grp
        if d == 1 and back >= 2:
            near = jnp.logical_and(near, jnp.logical_not(odd_near))
        return near

    hands_on = jnp.logical_and(relays, swapped)

    def hand_copy(b, which):
        src = pl.ds(pl.multiple_of((back - 2) * grp + b * tok, tok), tok)
        dst = pl.ds(pl.multiple_of((back - 1) * grp + b * tok, tok), tok)
        return pltpu.make_async_remote_copy(
            src_ref=kvbuf.at[1, which, src, :], dst_ref=kvbuf.at[1, which, dst, :],
            send_sem=hs.at[b, which], recv_sem=fr.at[1, b, which],
            device_id=(srv - G, z), device_id_type=MESH)

    def moved_wait(d, b, which):
        rows = pl.ds((back - d) * grp + b * tok, tok)
        ref = kvbuf.at[1, which, rows, :]
        pltpu.make_async_copy(ref, ref, fr.at[d, b, which]).wait()

    def pass_on(which):
        @pl.when(inner)
        def _():
            pltpu.make_async_copy(fkv.at[which], fkv.at[which], xr.at[which]).wait()
            for d in range(back, -1, -1):
                @pl.when(passes(d))
                def _():
                    pass_copy(d, which).start()

            @pl.when(swapped)
            def _():
                kvbuf[1, which, own_rows, :] = fkv[which]

    for which in range(2):
        if back >= 2:
            @pl.when(relays)
            def _():
                kv_wait(2, G - 1, which)
                relay_copy(G - 1, which).start()
        if swap:
            pass_on(which)

    def wait_moved():
        for which in range(2):
            for d in range(back + 1):
                for b in range(G):
                    if d == 0:
                        if b < G - 1:
                            moved_wait(d, b, which)
                    else:
                        ready = k - d >= 0
                        if d == 2:
                            ready = jnp.logical_and(ready, jnp.logical_not(relays))

                        @pl.when(ready)
                        def _():
                            moved_wait(d, b, which)

    def kv_wait_new(d, b, which):
        if (d, b) == (2, G - 1):
            @pl.when(jnp.logical_not(relays))
            def _():
                kv_wait(d, b, which)
        else:
            kv_wait(d, b, which)

    def wait_early(which):
        for i in range(1, G):
            kv_wait(0, (a + i) % G, which)
        for d in range(1, back + 1):
            @pl.when(k - d >= 0)
            def _():
                for b in range(G - 1 if d == back else 0, G):
                    kv_wait_new(d, b, which)

    def wait_late():
        @pl.when(k - back >= 0)
        def _():
            for b in range(G - 1):
                for which in range(2):
                    kv_wait_new(back, b, which)

    wait_early(0)

    edge = n_head // 4
    outer = jnp.logical_or(z < edge, z >= n_head - edge)
    scale = HEAD ** -0.5 * math.log2(math.e)

    def pick(blk, order):
        out = jnp.int32(order[-1])
        for i in range(len(order) - 1):
            out = jnp.where(blk == i, order[i], out)
        return out

    def order_of(blk):
        if nblk != 4:
            return blk
        def both(i):
            return jnp.where(k == 0, pick(blk, ORDS[3 + i]), pick(blk, ORDS[i]))

        outer_blk = jnp.where(mine_half == 0, both(0), both(2))
        low = jnp.logical_and(jnp.logical_and(inner, mine_half == 0), a < G - 1)
        return jnp.where(outer, outer_blk, jnp.where(low, both(1), blk))

    def where_of(u):
        blk = u // nch
        c = u % nch
        blk = order_of(blk)
        b = jnp.where(k == 0, blk % G, G - 1 - blk % G)
        slot = (mine_half + jnp.where(swapped, 0, 1) + blk // G) % nbm
        foreign = jnp.where(jnp.logical_and(swapped, slot != mine_half), 1, 0)
        part = jnp.where(foreign == 1, mine_half, slot)
        return c, b, slot, part, foreign

    def make_bias(u):
        c, b, slot, part, foreign = where_of(u)
        r0 = pl.multiple_of(b * tok + part * R, R)
        rows = k * grp + r0 + lax.broadcasted_iota(jnp.int32, (R, HEAD), 0)
        start = starts_of(rows)
        for j in range(W // HEAD):
            t = (k - back) * grp + r0 + j * HEAD + lax.broadcasted_iota(jnp.int32, (R, HEAD), 1)
            ok = jnp.logical_and(t >= start, t <= rows)
            bias[:, j * HEAD:(j + 1) * HEAD] = jnp.where(ok, 0.0, -1e30)

    def scores(u, sc, mx):
        c, b, slot, part, foreign = where_of(u)
        r0 = pl.multiple_of(b * tok + part * R, R)
        q0 = pl.multiple_of((b * nbm + slot) * R, R)
        kcol = pl.ds(pl.multiple_of((c * chunk // per) * HEAD, HEAD), HEAD)
        q = qrot[pl.ds(c * chunk, chunk), pl.ds(q0, R), :].reshape(rows_u, HEAD)
        top = None
        for t0 in range(0, W, 2 * HEAD):
            n = min(2 * HEAD, W - t0)
            keys = kvbuf[foreign, 0, pl.ds(pl.multiple_of(r0 + t0, HEAD), n), kcol]
            s = lax.dot_general(q, keys, (((1,), (1,)), ((), ())), preferred_element_type=jnp.float32)
            s = (s.reshape(chunk, R, n) + bias[:, t0:t0 + n][None]).reshape(rows_u, n)
            sc[:, t0:t0 + n] = s
            m = functools.reduce(jnp.maximum, [s[:, h:h + HEAD] for h in range(0, n, HEAD)])
            top = m if top is None else jnp.maximum(top, m)
        mx[...] = jnp.broadcast_to(jnp.max(top, axis=1, keepdims=True), (rows_u, HEAD))

    def attend(u, sc, mx):
        c, b, slot, part, foreign = where_of(u)
        r0 = pl.multiple_of(b * tok + part * R, R)
        kcol = pl.ds(pl.multiple_of((c * chunk // per) * HEAD, HEAD), HEAD)
        top = mx[...]
        acc = None
        for t0 in range(0, W, 2 * HEAD):
            n = min(2 * HEAD, W - t0)
            peak = jnp.concatenate([top] * (n // HEAD), axis=1)
            w = jnp.exp2((sc[:, t0:t0 + n] - peak) * scale).astype(jnp.bfloat16)
            vals = kvbuf[foreign, 1, pl.ds(pl.multiple_of(r0 + t0, HEAD), n), kcol]
            vals = jnp.concatenate([vals, jnp.ones_like(vals)], axis=1)
            part_acc = lax.dot_general(w, vals, (((1,), (0,)), ((), ())), preferred_element_type=jnp.float32)
            acc = part_acc if acc is None else acc + part_acc
        o = (acc[:, :HEAD] / acc[:, HEAD:]).astype(jnp.bfloat16)
        for h in range(chunk):
            obuf[u, :, h * HEAD:(h + 1) * HEAD] = o[h * R:(h + 1) * R, :]

    def out_copy(u, j):
        c, b, slot, part, foreign = where_of(u)
        dest = part * per_blk + j
        zsrc = jnp.where(foreign == 1, partner, z)
        col = pl.multiple_of(zsrc * (G * width) + a * width + c * cw, HEAD)
        src = obuf.at[u, pl.ds(j * T, T), :]
        dst = out_ref.at[:, pl.ds(col, cw)]
        idx = (zsrc * G + a) * nch + c
        remote = pltpu.make_async_remote_copy(
            src_ref=src, dst_ref=dst, send_sem=osend.at[u * per_blk + j], recv_sem=orecv.at[idx],
            device_id=(k * G + b, dest), device_id_type=MESH)
        local = pltpu.make_async_copy(src, dst, orecv.at[idx])
        mine = jnp.logical_and(b == a, dest == z)
        return mine, remote, local

    def held(u, j):
        if j < per_blk - 1 or nblk != 4 or per_blk < 2:
            return u < 0
        c, b, slot, part, foreign = where_of(u)
        plain = jnp.logical_not(swapped)
        return jnp.logical_and(jnp.logical_and(plain, jnp.logical_or(k == 0, u >= 2 * nch)), jnp.logical_and(mine_half == 1, part == 0))

    def send_out(u):
        for j in range(per_blk):
            mine, remote, local = out_copy(u, j)

            @pl.when(mine)
            def _():
                local.start()

            @pl.when(jnp.logical_not(jnp.logical_or(mine, held(u, j))))
            def _():
                remote.start()

    def send_held(i, carry):
        u = i

        @pl.when(held(u, per_blk - 1))
        def _():
            out_copy(u, per_blk - 1)[1].start()
        return carry

    def open_block(u):
        blk = u // nch

        @pl.when(blk == 1)
        def _():
            wait_late()

        if swap:
            @pl.when(jnp.logical_and(swapped, blk == nblk // nbm))
            def _():
                wait_moved()
                for b in range(G):
                    q_wait(b, nbm - 1 - mine_half)
                    rotate_queries(b, nbm - 1 - mine_half, mine_half)

        make_bias(u)

    make_bias(0)
    scores(0, sc0, mx0)
    wait_early(1)

    def one_step(u, carry):
        if swap and back >= 2:
            @pl.when(jnp.logical_and(hands_on, u == nch // 2))
            def _():
                for which in range(2):
                    for b in range(G):
                        moved_wait(2, b, which)
                        hand_copy(b, which).start()

        @pl.when(jnp.logical_and((u + 1) % nch == 0, u + 1 < units))
        def _():
            open_block(u + 1)

        attend(u, sc0, mx0)
        scores(jnp.minimum(u + 1, units - 1), sc0, mx0)
        send_out(u)
        return carry

    lax.fori_loop(0, units, one_step, 0)
    lax.fori_loop(0, units, send_held, 0)

    for i in range(1, G):
        for which in (1, 0):
            kv_copy(0, i, which).wait_send()
        for p in range(nbm):
            @pl.when(chip_kept(i, p))
            def _():
                chip_q(i, p).wait_send()
    for d in range(1, back + 1):
        @pl.when(sends(d))
        def _():
            for i in range(G):
                for which in (1, 0):
                    kv_copy(d, i, which).wait_send()
    if back >= 2:
        @pl.when(relays)
        def _():
            for which in range(2):
                relay_copy(G - 1, which).wait_send()
    if swap:
        @pl.when(inner)
        def _():
            if back >= 2:
                @pl.when(hands_on)
                def _():
                    for which in range(2):
                        for b in range(G):
                            hand_copy(b, which).wait_send()

            @pl.when(serves)
            def _():
                cross_q().wait_send()

            for which in range(2):
                cross_kv(which).wait_send()
                for d in range(back + 1):
                    @pl.when(passes(d))
                    def _():
                        pass_copy(d, which).wait_send()

    def end_send(u, carry):
        for j in range(per_blk):
            mine, remote, local = out_copy(u, j)

            @pl.when(jnp.logical_not(mine))
            def _():
                remote.wait_send()
        return carry

    lax.fori_loop(0, units, end_send, 0)

    def end_recv(i, carry):
        col = pl.multiple_of(i * cw, HEAD)
        ref = out_ref.at[:, pl.ds(col, cw)]
        pltpu.make_async_copy(ref, ref, orecv.at[i]).wait()
        return carry

    lax.fori_loop(0, n_head * G * nch, end_recv, 0)


def solution(mesh):
    n_srv, n_head = mesh.shape["srv"], mesh.shape["head"]

    def body(queries, key_value_pair, lengths):
        tok, qw = queries.shape
        kv_all = key_value_pair.shape[2] // HEAD
        G = 2 if kv_all % 2 == 0 and n_srv % 2 == 0 else 1
        kvh = kv_all // G
        per = qw // HEAD // kv_all
        grp = G * tok
        n_grp = n_srv // G
        back = n_grp // 2
        T = tok // n_head
        R = max(tok // 2, T)
        chunk = per // 4
        ndoc = lengths.shape[0]
        heads = kvh * per
        nch = heads // chunk
        units = (grp // R) * nch
        W = back * grp + R
        swap = True and G == 2 and n_head % 2 == 0 and tok // R == 2
        cfg = (n_srv, n_head, G, back, tok, kvh, per, R, chunk, ndoc, swap)
        bf = jnp.bfloat16
        dma = pltpu.SemaphoreType.DMA
        return pl.pallas_call(
            functools.partial(kernel, cfg),
            out_shape=pltpu.VMEM((T, qw * n_head), bf),
            in_specs=[
                pl.BlockSpec(memory_space=pltpu.SMEM),
                pl.BlockSpec(memory_space=pl.ANY),
                pl.BlockSpec(memory_space=pl.ANY),
            ],
            out_specs=pl.BlockSpec(memory_space=pl.ANY),
            scratch_shapes=[
                pltpu.VMEM((G, tok // R, R, heads * HEAD), bf),
                pltpu.VMEM((heads, grp, HEAD), bf),
                pltpu.VMEM((2, 2, (back + 1) * grp, kvh * HEAD), bf),
                pltpu.VMEM((2, tok, kv_all * HEAD), bf),
                pltpu.VMEM((tok, kv_all * HEAD), bf),
                pltpu.VMEM((2, tok, kvh * HEAD), bf),
                pltpu.VMEM((G, 2, tok, HEAD), jnp.float32),
                pltpu.VMEM((R, W), jnp.float32),
                pltpu.VMEM((chunk * R, W), jnp.float32),
                pltpu.VMEM((chunk * R, HEAD), jnp.float32),
                pltpu.VMEM((units, R, chunk * HEAD), bf),
                dma((1,)),
                dma((G, tok // R)),
                dma((G, tok // R)),
                dma((back + 1, G, 2)),
                dma((back + 1, G, 2)),
                dma((G, 2)),
                dma((3,)),
                dma((2,)),
                dma((back + 1, 2)),
                dma((back + 1, G, 2)),
                dma((G, 2)),
                dma((units * (R // T),)),
                dma((n_head * G * nch,)),
            ],
            compiler_params=pltpu.CompilerParams(collective_id=0, has_side_effects=True),
            name="attend",
        )(lengths, queries, key_value_pair)

    in_specs = (P("srv", "head"), P(None, "srv", "head"), P())
    out_specs = P(("srv", "head"), None)
    return jax.shard_map(body, mesh=mesh, in_specs=in_specs, out_specs=out_specs, check_vma=False)
```

```python
import functools
import math

import jax
import jax.numpy as jnp
from jax import lax
from jax.experimental import pallas as pl
from jax.experimental.pallas import tpu as pltpu
from jax.sharding import PartitionSpec as P

HEAD = 128
ORDS = ((0, 2, 3, 1), (2, 0, 1, 3), (0, 2, 3, 1), (0, 2, 3, 1), (2, 3, 0, 1), (0, 2, 3, 1))
MESH = pl.DeviceIdType.MESH


def kernel(cfg, len_ref, q_ref, kv_ref, out_ref, qraw, qrot, kvbuf, kvin, ksend, fkv, table, bias,
           sc0, mx0, obuf, lsem, qs, qr, kvs, kvr, fwd, xs, xr, fs, fr, hs, far, osend, orecv):
    n_srv, n_head, G, back, tok, kvh, per, R, chunk, ndoc, swap = cfg
    heads = kvh * per
    grp = G * tok
    n_grp = n_srv // G
    T = tok // n_head
    longest = back * grp
    W = longest + R
    width = heads * HEAD
    kw = kvh * HEAD
    nbm = tok // R
    nblk = grp // R
    nch = heads // chunk
    units = nblk * nch
    per_blk = R // T
    cw = chunk * HEAD
    rows_u = chunk * R
    srv = lax.axis_index("srv")
    z = lax.axis_index("head")
    k = srv // G
    a = srv % G

    mine_half = z // (n_head // nbm)
    partner = n_head - 1 - z
    if swap:
        inner = jnp.logical_or(z == n_head // 2 - 1, z == n_head // 2)
    else:
        inner = z < 0
    serves = inner
    swapped = jnp.logical_and(serves, a == G - 1)

    bar = pltpu.get_barrier_semaphore()

    own_kv = pltpu.make_async_copy(kv_ref, kvin, lsem.at[0])
    own_kv.start()

    def cols_of(b):
        return pl.ds(pl.multiple_of(b * width, HEAD), width)

    def part_rows(p):
        return slice(p * R, (p + 1) * R)

    def own_q(p):
        return pltpu.make_async_copy(q_ref.at[part_rows(p), cols_of(a)], qraw.at[a, p], qr.at[a, p])

    def kept(p):
        return jnp.logical_not(jnp.logical_and(swapped, mine_half != p))

    for p in range(nbm):
        @pl.when(kept(p))
        def _():
            own_q(p).start()

    def greet(s, h):
        pl.semaphore_signal(bar, inc=1, device_id=(s, h), device_id_type=MESH)

    chain = swap and n_head == 4
    outward = jnp.where(mine_half == 0, 0, n_head - 1)
    if chain:
        @pl.when(inner)
        def _():
            for b in range(G):
                greet(k * G + b, partner)
                greet(k * G + b, outward)

        @pl.when(jnp.logical_not(inner))
        def _():
            for b in range(G):
                greet(k * G + b, jnp.where(mine_half == 0, 1, n_head - 2))
    else:
        for i in range(1, n_head):
            for b in range(G):
                greet(k * G + b, (z + i) % n_head)
    for i in range(1, G):
        greet(k * G + (a + i) % G, z)
    for d in range(1, back + 1):
        @pl.when(k + d < n_grp)
        def _():
            for b in range(G):
                greet((k + d) * G + b, z)

        @pl.when(k - d >= 0)
        def _():
            for b in range(G):
                greet((k - d) * G + b, z)

    ends = []
    total = jnp.int32(0)
    for i in range(ndoc):
        total = total + len_ref[i]
        ends.append(total)

    lane = lax.broadcasted_iota(jnp.int32, (tok, HEAD), 1)
    low = lane < HEAD // 2
    step_up = jnp.where(low, lane, lane - HEAD // 2).astype(jnp.float32) * (2.0 / HEAD)
    inverse = jnp.exp(-step_up * math.log(500000.0))

    def starts_of(rows):
        start = jnp.zeros_like(rows)
        for e in ends:
            start = jnp.where(e <= rows, e, start)
        return start

    def cos_sin(angle):
        turns = jnp.floor(angle * (2.0 / math.pi) + 0.5)
        r = ((angle - turns * 1.5703125) - turns * 4.837512969970703125e-4) - turns * 7.549789948768648e-8
        r2 = r * r
        s = r + r * r2 * (-1.6666654611e-1 + r2 * (8.3321608736e-3 - r2 * 1.9515295891e-4))
        c = 1.0 - 0.5 * r2 + r2 * r2 * (
            4.166664568298827e-2 + r2 * (-1.388731625493765e-3 + r2 * 2.443315711809948e-5))
        quarter = turns.astype(jnp.int32)
        odd = (quarter & 1) == 1
        sine = jnp.where(odd, c, s)
        cosine = jnp.where(odd, s, c)
        sine = jnp.where((quarter & 2) == 2, -sine, sine)
        cosine = jnp.where(((quarter + 1) & 2) == 2, -cosine, cosine)
        return cosine, sine

    def make_table(b):
        rows = (k * G + b) * tok + lax.broadcasted_iota(jnp.int32, (tok, HEAD), 0)
        angle = (rows - starts_of(rows)).astype(jnp.float32) * inverse
        cosine, sine = cos_sin(angle)
        table[b, 0] = cosine
        table[b, 1] = jnp.where(low, -sine, sine)

    def rotate(x, cosine, sine):
        x = x.astype(jnp.float32)
        return (x * cosine + pltpu.roll(x, HEAD // 2, 1) * sine).astype(jnp.bfloat16)

    make_table(a)
    own_kv.wait()
    for h in range(G * kvh):
        cols = slice(h * HEAD, (h + 1) * HEAD)
        ksend[:, cols] = rotate(kvin[0, :, cols], table[a, 0], table[a, 1])

    own_rows = pl.ds(pl.multiple_of(back * grp + a * tok, tok), tok)
    kv_cols = pl.ds(pl.multiple_of(a * kw, HEAD), kw)
    kvbuf[0, 0, own_rows, :] = ksend[:, kv_cols]
    kvbuf[0, 1, own_rows, :] = kvin[1, :, kv_cols]

    count = (jnp.where(inner, 2, 1) if chain else n_head - 1) * G + (G - 1)
    for d in range(1, back + 1):
        count = count + G * jnp.where(k + d < n_grp, 1, 0) + G * jnp.where(k - d >= 0, 1, 0)
    pl.semaphore_wait(bar, count)

    def tell(h):
        pl.semaphore_signal(far, inc=1, device_id=(srv, h), device_id_type=MESH)

    if chain:
        @pl.when(inner)
        def _():
            tell(partner)
            tell(outward)

    def kv_copy(d, i, which):
        b = (a + i) % G
        cols = pl.ds(pl.multiple_of(b * kw, HEAD), kw)
        src = ksend.at[:, cols] if which == 0 else kvin.at[1, :, cols]
        rows = pl.ds(pl.multiple_of((back - d) * grp + a * tok, tok), tok)
        return pltpu.make_async_remote_copy(
            src_ref=src, dst_ref=kvbuf.at[0, which, rows, :],
            send_sem=kvs.at[d, i, which], recv_sem=kvr.at[d, a, which],
            device_id=((k + d) * G + b, z), device_id_type=MESH)

    def kv_wait(d, b, which):
        rows = pl.ds(pl.multiple_of((back - d) * grp + b * tok, tok), tok)
        ref = kvbuf.at[0, which, rows, :]
        pltpu.make_async_copy(ref, ref, kvr.at[d, b, which]).wait()

    odd_near = jnp.logical_and(k % 2 == 1, k + 2 < n_grp)
    relayed = jnp.logical_and(odd_near, a == G - 1)
    relays = jnp.logical_and(k % 2 == 1, k >= 3)

    def sends(d):
        near = k + d < n_grp
        if d == 1 and back >= 2:
            near = jnp.logical_and(near, jnp.logical_not(relayed))
        return near

    def relay_copy(b, which):
        src = pl.ds(pl.multiple_of((back - 2) * grp + b * tok, tok), tok)
        dst = pl.ds(pl.multiple_of((back - 1) * grp + b * tok, tok), tok)
        return pltpu.make_async_remote_copy(
            src_ref=kvbuf.at[0, which, src, :], dst_ref=kvbuf.at[0, which, dst, :],
            send_sem=fwd.at[b, which], recv_sem=kvr.at[1, b, which],
            device_id=(srv - G, z), device_id_type=MESH)

    def start_kv(d, when):
        @pl.when(jnp.logical_and(sends(d), when))
        def _():
            pairs = [(i, which) for which in range(2) for i in range(G)]
            for i, which in pairs if d == 1 else sorted(pairs):
                kv_copy(d, i, which).start()

    moved = pl.ds((G - 1) * kw, kw)

    def cross_kv(which):
        src = ksend.at[:, moved] if which == 0 else kvin.at[1, :, moved]
        return pltpu.make_async_remote_copy(
            src_ref=src, dst_ref=fkv.at[which], send_sem=xs.at[which], recv_sem=xr.at[which],
            device_id=(srv, partner), device_id_type=MESH)

    def cross_q():
        there = nbm - 1 - mine_half
        src = pl.ds(pl.multiple_of(there * R, R), R)
        return pltpu.make_async_remote_copy(
            src_ref=q_ref.at[src, pl.ds((G - 1) * width, width)], dst_ref=qraw.at[a, mine_half],
            send_sem=xs.at[2], recv_sem=qr.at[a, mine_half],
            device_id=(k * G + G - 1, partner), device_id_type=MESH)

    def chip_q(i, p):
        b = (a + i) % G
        return pltpu.make_async_remote_copy(
            src_ref=q_ref.at[part_rows(p), cols_of(b)], dst_ref=qraw.at[a, p],
            send_sem=qs.at[i, p], recv_sem=qr.at[a, p],
            device_id=(k * G + b, z), device_id_type=MESH)

    def chip_kept(i, p):
        b = (a + i) % G
        away = jnp.logical_and(jnp.logical_and(serves, b == G - 1), mine_half != p)
        return jnp.logical_not(away)

    if swap:
        @pl.when(inner)
        def _():
            cross_kv(0).start()
            cross_kv(1).start()
            cross_q().start()
    for d in range(1, back + 1):
        start_kv(d, a == G - 1 if d == back else True)
    for i in range(1, G):
        for which in range(2):
            kv_copy(0, i, which).start()
        for p in range(nbm):
            @pl.when(chip_kept(i, p))
            def _():
                chip_q(i, p).start()

    def q_wait(b, p):
        pltpu.make_async_copy(qraw.at[b, p], qraw.at[b, p], qr.at[b, p]).wait()

    def rotate_queries(b, p, part):
        rows = pl.ds(pl.multiple_of(part * R, R), R)
        cosine = table[b, 0, rows, :]
        sine = table[b, 1, rows, :]
        dst = pl.ds(pl.multiple_of((b * nbm + p) * R, R), R)
        for h in range(heads):
            qrot[h, dst, :] = rotate(qraw[b, p, :, h * HEAD:(h + 1) * HEAD], cosine, sine)

    def take_queries(b):
        for p in range(nbm):
            @pl.when(kept(p))
            def _():
                q_wait(b, p)
                rotate_queries(b, p, p)

    for d in range(1, back + 1):
        @pl.when(k - d < 0)
        def _():
            for sel in range(2 if swap else 1):
                kvbuf[sel, :, pl.ds((back - d) * grp, grp), :] = jnp.zeros((2, grp, kw), jnp.bfloat16)

    take_queries(a)
    for i in range(1, G):
        b = (a + i) % G
        make_table(b)
        take_queries(b)

    start_kv(back, a < G - 1)
    def pass_copy(d, which):
        rows = pl.ds(pl.multiple_of((back - d) * grp + a * tok, tok), tok)
        return pltpu.make_async_remote_copy(
            src_ref=fkv.at[which], dst_ref=kvbuf.at[1, which, rows, :],
            send_sem=fs.at[d, which], recv_sem=fr.at[d, a, which],
            device_id=((k + d) * G + G - 1, z), device_id_type=MESH)

    def passes(d):
        if d == 0:
            return a < G - 1
        near = k + d < n_grp
        if d == 1 and back >= 2:
            near = jnp.logical_and(near, jnp.logical_not(odd_near))
        return near

    hands_on = jnp.logical_and(relays, swapped)

    def hand_copy(b, which):
        src = pl.ds(pl.multiple_of((back - 2) * grp + b * tok, tok), tok)
        dst = pl.ds(pl.multiple_of((back - 1) * grp + b * tok, tok), tok)
        return pltpu.make_async_remote_copy(
            src_ref=kvbuf.at[1, which, src, :], dst_ref=kvbuf.at[1, which, dst, :],
            send_sem=hs.at[b, which], recv_sem=fr.at[1, b, which],
            device_id=(srv - G, z), device_id_type=MESH)

    def moved_wait(d, b, which):
        rows = pl.ds((back - d) * grp + b * tok, tok)
        ref = kvbuf.at[1, which, rows, :]
        pltpu.make_async_copy(ref, ref, fr.at[d, b, which]).wait()

    def pass_on(which):
        @pl.when(inner)
        def _():
            pltpu.make_async_copy(fkv.at[which], fkv.at[which], xr.at[which]).wait()
            for d in range(back, -1, -1):
                @pl.when(passes(d))
                def _():
                    pass_copy(d, which).start()

            @pl.when(swapped)
            def _():
                kvbuf[1, which, own_rows, :] = fkv[which]

    for which in range(2):
        if back >= 2:
            @pl.when(relays)
            def _():
                kv_wait(2, G - 1, which)
                relay_copy(G - 1, which).start()
        if swap:
            pass_on(which)

    def wait_moved():
        for which in range(2):
            for d in range(back + 1):
                for b in range(G):
                    if d == 0:
                        if b < G - 1:
                            moved_wait(d, b, which)
                    else:
                        ready = k - d >= 0
                        if d == 2:
                            ready = jnp.logical_and(ready, jnp.logical_not(relays))

                        @pl.when(ready)
                        def _():
                            moved_wait(d, b, which)

    def kv_wait_new(d, b, which):
        if (d, b) == (2, G - 1):
            @pl.when(jnp.logical_not(relays))
            def _():
                kv_wait(d, b, which)
        else:
            kv_wait(d, b, which)

    def wait_early(which):
        for i in range(1, G):
            kv_wait(0, (a + i) % G, which)
        for d in range(1, back + 1):
            @pl.when(k - d >= 0)
            def _():
                for b in range(G - 1 if d == back else 0, G):
                    kv_wait_new(d, b, which)

    def wait_late():
        @pl.when(k - back >= 0)
        def _():
            for b in range(G - 1):
                for which in range(2):
                    kv_wait_new(back, b, which)

    if chain:
        @pl.when(inner)
        def _():
            pl.semaphore_wait(far, 1)
            tell(outward)

        @pl.when(jnp.logical_not(inner))
        def _():
            pl.semaphore_wait(far, 2)

    wait_early(0)

    edge = n_head // 4
    outer = jnp.logical_or(z < edge, z >= n_head - edge)
    scale = HEAD ** -0.5 * math.log2(math.e)

    def pick(blk, order):
        out = jnp.int32(order[-1])
        for i in range(len(order) - 1):
            out = jnp.where(blk == i, order[i], out)
        return out

    def order_of(blk):
        if nblk != 4:
            return blk
        def both(i):
            return jnp.where(k == 0, pick(blk, ORDS[3 + i]), pick(blk, ORDS[i]))

        outer_blk = jnp.where(mine_half == 0, both(0), both(2))
        low = jnp.logical_and(jnp.logical_and(inner, mine_half == 0), a < G - 1)
        return jnp.where(outer, outer_blk, jnp.where(low, both(1), blk))

    def where_of(u):
        blk = u // nch
        c = u % nch
        blk = order_of(blk)
        b = jnp.where(k == 0, blk % G, G - 1 - blk % G)
        slot = (mine_half + jnp.where(swapped, 0, 1) + blk // G) % nbm
        foreign = jnp.where(jnp.logical_and(swapped, slot != mine_half), 1, 0)
        part = jnp.where(foreign == 1, mine_half, slot)
        return c, b, slot, part, foreign

    def make_bias(u):
        c, b, slot, part, foreign = where_of(u)
        r0 = pl.multiple_of(b * tok + part * R, R)
        rows = k * grp + r0 + lax.broadcasted_iota(jnp.int32, (R, HEAD), 0)
        start = starts_of(rows)
        for j in range(W // HEAD):
            t = (k - back) * grp + r0 + j * HEAD + lax.broadcasted_iota(jnp.int32, (R, HEAD), 1)
            ok = jnp.logical_and(t >= start, t <= rows)
            bias[:, j * HEAD:(j + 1) * HEAD] = jnp.where(ok, 0.0, -1e30)

    def scores(u, sc, mx):
        c, b, slot, part, foreign = where_of(u)
        r0 = pl.multiple_of(b * tok + part * R, R)
        q0 = pl.multiple_of((b * nbm + slot) * R, R)
        kcol = pl.ds(pl.multiple_of((c * chunk // per) * HEAD, HEAD), HEAD)
        q = qrot[pl.ds(c * chunk, chunk), pl.ds(q0, R), :].reshape(rows_u, HEAD)
        top = None
        for t0 in range(0, W, 2 * HEAD):
            n = min(2 * HEAD, W - t0)
            keys = kvbuf[foreign, 0, pl.ds(pl.multiple_of(r0 + t0, HEAD), n), kcol]
            s = lax.dot_general(q, keys, (((1,), (1,)), ((), ())), preferred_element_type=jnp.float32)
            s = (s.reshape(chunk, R, n) + bias[:, t0:t0 + n][None]).reshape(rows_u, n)
            sc[:, t0:t0 + n] = s
            m = functools.reduce(jnp.maximum, [s[:, h:h + HEAD] for h in range(0, n, HEAD)])
            top = m if top is None else jnp.maximum(top, m)
        mx[...] = jnp.broadcast_to(jnp.max(top, axis=1, keepdims=True), (rows_u, HEAD))

    def attend(u, sc, mx):
        c, b, slot, part, foreign = where_of(u)
        r0 = pl.multiple_of(b * tok + part * R, R)
        kcol = pl.ds(pl.multiple_of((c * chunk // per) * HEAD, HEAD), HEAD)
        top = mx[...]
        acc = None
        for t0 in range(0, W, 2 * HEAD):
            n = min(2 * HEAD, W - t0)
            peak = jnp.concatenate([top] * (n // HEAD), axis=1)
            w = jnp.exp2((sc[:, t0:t0 + n] - peak) * scale).astype(jnp.bfloat16)
            vals = kvbuf[foreign, 1, pl.ds(pl.multiple_of(r0 + t0, HEAD), n), kcol]
            vals = jnp.concatenate([vals, jnp.ones_like(vals)], axis=1)
            part_acc = lax.dot_general(w, vals, (((1,), (0,)), ((), ())), preferred_element_type=jnp.float32)
            acc = part_acc if acc is None else acc + part_acc
        o = (acc[:, :HEAD] / acc[:, HEAD:]).astype(jnp.bfloat16)
        for h in range(chunk):
            obuf[u, :, h * HEAD:(h + 1) * HEAD] = o[h * R:(h + 1) * R, :]

    def out_copy(u, j):
        c, b, slot, part, foreign = where_of(u)
        dest = part * per_blk + j
        zsrc = jnp.where(foreign == 1, partner, z)
        col = pl.multiple_of(zsrc * (G * width) + a * width + c * cw, HEAD)
        src = obuf.at[u, pl.ds(j * T, T), :]
        dst = out_ref.at[:, pl.ds(col, cw)]
        idx = (zsrc * G + a) * nch + c
        remote = pltpu.make_async_remote_copy(
            src_ref=src, dst_ref=dst, send_sem=osend.at[u * per_blk + j], recv_sem=orecv.at[idx],
            device_id=(k * G + b, dest), device_id_type=MESH)
        local = pltpu.make_async_copy(src, dst, orecv.at[idx])
        mine = jnp.logical_and(b == a, dest == z)
        return mine, remote, local

    def held(u, j):
        if j < per_blk - 1 or nblk != 4 or per_blk < 2:
            return u < 0
        c, b, slot, part, foreign = where_of(u)
        plain = jnp.logical_not(swapped)
        return jnp.logical_and(jnp.logical_and(plain, u >= jnp.where(k == 0, nch, 2 * nch)), jnp.logical_and(mine_half == 1, part == 0))

    def send_out(u):
        for j in range(per_blk):
            mine, remote, local = out_copy(u, j)

            @pl.when(mine)
            def _():
                local.start()

            @pl.when(jnp.logical_not(jnp.logical_or(mine, held(u, j))))
            def _():
                remote.start()

    def send_held(i, carry):
        u = i

        @pl.when(held(u, per_blk - 1))
        def _():
            out_copy(u, per_blk - 1)[1].start()
        return carry

    def open_block(u):
        blk = u // nch

        @pl.when(blk == 1)
        def _():
            wait_late()

        if swap:
            @pl.when(jnp.logical_and(swapped, blk == nblk // nbm))
            def _():
                wait_moved()
                for b in range(G):
                    q_wait(b, nbm - 1 - mine_half)
                    rotate_queries(b, nbm - 1 - mine_half, mine_half)

        make_bias(u)

    make_bias(0)
    scores(0, sc0, mx0)
    wait_early(1)

    def one_step(u, carry):
        if swap and back >= 2:
            @pl.when(jnp.logical_and(hands_on, u == nch // 2))
            def _():
                for which in range(2):
                    for b in range(G):
                        moved_wait(2, b, which)
                        hand_copy(b, which).start()

        @pl.when(jnp.logical_and((u + 1) % nch == 0, u + 1 < units))
        def _():
            open_block(u + 1)

        attend(u, sc0, mx0)
        scores(jnp.minimum(u + 1, units - 1), sc0, mx0)
        send_out(u)
        return carry

    lax.fori_loop(0, units, one_step, 0)
    lax.fori_loop(0, units, send_held, 0)

    for i in range(1, G):
        for which in (1, 0):
            kv_copy(0, i, which).wait_send()
        for p in range(nbm):
            @pl.when(chip_kept(i, p))
            def _():
                chip_q(i, p).wait_send()
    for d in range(1, back + 1):
        @pl.when(sends(d))
        def _():
            for i in range(G):
                for which in (1, 0):
                    kv_copy(d, i, which).wait_send()
    if back >= 2:
        @pl.when(relays)
        def _():
            for which in range(2):
                relay_copy(G - 1, which).wait_send()
    if swap:
        @pl.when(inner)
        def _():
            if back >= 2:
                @pl.when(hands_on)
                def _():
                    for which in range(2):
                        for b in range(G):
                            hand_copy(b, which).wait_send()

            @pl.when(serves)
            def _():
                cross_q().wait_send()

            for which in range(2):
                cross_kv(which).wait_send()
                for d in range(back + 1):
                    @pl.when(passes(d))
                    def _():
                        pass_copy(d, which).wait_send()

    def end_send(u, carry):
        for j in range(per_blk):
            mine, remote, local = out_copy(u, j)

            @pl.when(jnp.logical_not(mine))
            def _():
                remote.wait_send()
        return carry

    lax.fori_loop(0, units, end_send, 0)

    def end_recv(i, carry):
        col = pl.multiple_of(i * cw, HEAD)
        ref = out_ref.at[:, pl.ds(col, cw)]
        pltpu.make_async_copy(ref, ref, orecv.at[i]).wait()
        return carry

    lax.fori_loop(0, n_head * G * nch, end_recv, 0)


def solution(mesh):
    n_srv, n_head = mesh.shape["srv"], mesh.shape["head"]

    def body(queries, key_value_pair, lengths):
        tok, qw = queries.shape
        kv_all = key_value_pair.shape[2] // HEAD
        G = 2 if kv_all % 2 == 0 and n_srv % 2 == 0 else 1
        kvh = kv_all // G
        per = qw // HEAD // kv_all
        grp = G * tok
        n_grp = n_srv // G
        back = n_grp // 2
        T = tok // n_head
        R = max(tok // 2, T)
        chunk = per // 4
        ndoc = lengths.shape[0]
        heads = kvh * per
        nch = heads // chunk
        units = (grp // R) * nch
        W = back * grp + R
        swap = True and G == 2 and n_head % 2 == 0 and tok // R == 2
        cfg = (n_srv, n_head, G, back, tok, kvh, per, R, chunk, ndoc, swap)
        bf = jnp.bfloat16
        dma = pltpu.SemaphoreType.DMA
        return pl.pallas_call(
            functools.partial(kernel, cfg),
            out_shape=pltpu.VMEM((T, qw * n_head), bf),
            in_specs=[
                pl.BlockSpec(memory_space=pltpu.SMEM),
                pl.BlockSpec(memory_space=pl.ANY),
                pl.BlockSpec(memory_space=pl.ANY),
            ],
            out_specs=pl.BlockSpec(memory_space=pl.ANY),
            scratch_shapes=[
                pltpu.VMEM((G, tok // R, R, heads * HEAD), bf),
                pltpu.VMEM((heads, grp, HEAD), bf),
                pltpu.VMEM((2, 2, (back + 1) * grp, kvh * HEAD), bf),
                pltpu.VMEM((2, tok, kv_all * HEAD), bf),
                pltpu.VMEM((tok, kv_all * HEAD), bf),
                pltpu.VMEM((2, tok, kvh * HEAD), bf),
                pltpu.VMEM((G, 2, tok, HEAD), jnp.float32),
                pltpu.VMEM((R, W), jnp.float32),
                pltpu.VMEM((chunk * R, W), jnp.float32),
                pltpu.VMEM((chunk * R, HEAD), jnp.float32),
                pltpu.VMEM((units, R, chunk * HEAD), bf),
                dma((1,)),
                dma((G, tok // R)),
                dma((G, tok // R)),
                dma((back + 1, G, 2)),
                dma((back + 1, G, 2)),
                dma((G, 2)),
                dma((3,)),
                dma((2,)),
                dma((back + 1, 2)),
                dma((back + 1, G, 2)),
                dma((G, 2)),
                pltpu.SemaphoreType.REGULAR,
                dma((units * (R // T),)),
                dma((n_head * G * nch,)),
            ],
            compiler_params=pltpu.CompilerParams(collective_id=0, has_side_effects=True),
            name="attend",
        )(lengths, queries, key_value_pair)

    in_specs = (P("srv", "head"), P(None, "srv", "head"), P())
    out_specs = P(("srv", "head"), None)
    return jax.shard_map(body, mesh=mesh, in_specs=in_specs, out_specs=out_specs, check_vma=False)
```

```python
import functools
import math

import jax
import jax.numpy as jnp
from jax import lax
from jax.experimental import pallas as pl
from jax.experimental.pallas import tpu as pltpu
from jax.sharding import PartitionSpec as P

HEAD = 128
ORDS = ((0, 2, 3, 1), (2, 0, 1, 3), (0, 2, 3, 1), (0, 2, 3, 1), (2, 3, 0, 1), (0, 2, 3, 1))
MESH = pl.DeviceIdType.MESH


def kernel(cfg, len_ref, q_ref, kv_ref, out_ref, qraw, qrot, kvbuf, kvin, ksend, fkv, table, bias,
           sc0, mx0, obuf, lsem, qs, qr, kvs, kvr, fwd, xs, xr, fs, fr, hs, far, osend, orecv):
    n_srv, n_head, G, back, tok, kvh, per, R, chunk, ndoc, swap = cfg
    heads = kvh * per
    grp = G * tok
    n_grp = n_srv // G
    T = tok // n_head
    longest = back * grp
    W = longest + R
    width = heads * HEAD
    kw = kvh * HEAD
    nbm = tok // R
    nblk = grp // R
    nch = heads // chunk
    units = nblk * nch
    per_blk = R // T
    cw = chunk * HEAD
    rows_u = chunk * R
    srv = lax.axis_index("srv")
    z = lax.axis_index("head")
    k = srv // G
    a = srv % G

    mine_half = z // (n_head // nbm)
    partner = n_head - 1 - z
    if swap:
        inner = jnp.logical_or(z == n_head // 2 - 1, z == n_head // 2)
    else:
        inner = z < 0
    serves = inner
    swapped = jnp.logical_and(serves, a == G - 1)

    bar = pltpu.get_barrier_semaphore()

    own_kv = pltpu.make_async_copy(kv_ref, kvin, lsem.at[0])
    own_kv.start()

    def cols_of(b):
        return pl.ds(pl.multiple_of(b * width, HEAD), width)

    def part_rows(p):
        return slice(p * R, (p + 1) * R)

    def own_q(p):
        return pltpu.make_async_copy(q_ref.at[part_rows(p), cols_of(a)], qraw.at[a, p], qr.at[a, p])

    def kept(p):
        return jnp.logical_not(jnp.logical_and(swapped, mine_half != p))

    for p in range(nbm):
        @pl.when(kept(p))
        def _():
            own_q(p).start()

    def greet(s, h):
        pl.semaphore_signal(bar, inc=1, device_id=(s, h), device_id_type=MESH)

    chain = swap and n_head == 4
    outward = jnp.where(mine_half == 0, 0, n_head - 1)
    first_inner = z == n_head // 2 - 1
    if chain:
        for b in range(G):
            @pl.when(z < n_head - 1)
            def _():
                greet(k * G + b, z + 1)

            @pl.when(z == n_head // 2)
            def _():
                greet(k * G + b, z - 1)
    else:
        for i in range(1, n_head):
            for b in range(G):
                greet(k * G + b, (z + i) % n_head)
    for i in range(1, G):
        greet(k * G + (a + i) % G, z)
    for d in range(1, back + 1):
        @pl.when(k + d < n_grp)
        def _():
            for b in range(G):
                greet((k + d) * G + b, z)

        @pl.when(k - d >= 0)
        def _():
            for b in range(G):
                greet((k - d) * G + b, z)

    ends = []
    total = jnp.int32(0)
    for i in range(ndoc):
        total = total + len_ref[i]
        ends.append(total)

    lane = lax.broadcasted_iota(jnp.int32, (tok, HEAD), 1)
    low = lane < HEAD // 2
    step_up = jnp.where(low, lane, lane - HEAD // 2).astype(jnp.float32) * (2.0 / HEAD)
    inverse = jnp.exp(-step_up * math.log(500000.0))

    def starts_of(rows):
        start = jnp.zeros_like(rows)
        for e in ends:
            start = jnp.where(e <= rows, e, start)
        return start

    def cos_sin(angle):
        turns = jnp.floor(angle * (2.0 / math.pi) + 0.5)
        r = ((angle - turns * 1.5703125) - turns * 4.837512969970703125e-4) - turns * 7.549789948768648e-8
        r2 = r * r
        s = r + r * r2 * (-1.6666654611e-1 + r2 * (8.3321608736e-3 - r2 * 1.9515295891e-4))
        c = 1.0 - 0.5 * r2 + r2 * r2 * (
            4.166664568298827e-2 + r2 * (-1.388731625493765e-3 + r2 * 2.443315711809948e-5))
        quarter = turns.astype(jnp.int32)
        odd = (quarter & 1) == 1
        sine = jnp.where(odd, c, s)
        cosine = jnp.where(odd, s, c)
        sine = jnp.where((quarter & 2) == 2, -sine, sine)
        cosine = jnp.where(((quarter + 1) & 2) == 2, -cosine, cosine)
        return cosine, sine

    def make_table(b):
        rows = (k * G + b) * tok + lax.broadcasted_iota(jnp.int32, (tok, HEAD), 0)
        angle = (rows - starts_of(rows)).astype(jnp.float32) * inverse
        cosine, sine = cos_sin(angle)
        table[b, 0] = cosine
        table[b, 1] = jnp.where(low, -sine, sine)

    def rotate(x, cosine, sine):
        x = x.astype(jnp.float32)
        return (x * cosine + pltpu.roll(x, HEAD // 2, 1) * sine).astype(jnp.bfloat16)

    make_table(a)
    own_kv.wait()
    for h in range(G * kvh):
        cols = slice(h * HEAD, (h + 1) * HEAD)
        ksend[:, cols] = rotate(kvin[0, :, cols], table[a, 0], table[a, 1])

    own_rows = pl.ds(pl.multiple_of(back * grp + a * tok, tok), tok)
    kv_cols = pl.ds(pl.multiple_of(a * kw, HEAD), kw)
    kvbuf[0, 0, own_rows, :] = ksend[:, kv_cols]
    kvbuf[0, 1, own_rows, :] = kvin[1, :, kv_cols]

    if chain:
        count = jnp.where(first_inner, 2, jnp.where(z == 0, 0, 1)) * G + (G - 1)
    else:
        count = (n_head - 1) * G + (G - 1)
    for d in range(1, back + 1):
        count = count + G * jnp.where(k + d < n_grp, 1, 0) + G * jnp.where(k - d >= 0, 1, 0)
    pl.semaphore_wait(bar, count)

    def tell(h):
        pl.semaphore_signal(far, inc=1, device_id=(srv, h), device_id_type=MESH)

    def say_in():
        @pl.when(first_inner)
        def _():
            tell(0)
            tell(z + 1)

        @pl.when(z == n_head - 1)
        def _():
            tell(z - 1)

    def kv_copy(d, i, which):
        b = (a + i) % G
        cols = pl.ds(pl.multiple_of(b * kw, HEAD), kw)
        src = ksend.at[:, cols] if which == 0 else kvin.at[1, :, cols]
        rows = pl.ds(pl.multiple_of((back - d) * grp + a * tok, tok), tok)
        return pltpu.make_async_remote_copy(
            src_ref=src, dst_ref=kvbuf.at[0, which, rows, :],
            send_sem=kvs.at[d, i, which], recv_sem=kvr.at[d, a, which],
            device_id=((k + d) * G + b, z), device_id_type=MESH)

    def kv_wait(d, b, which):
        rows = pl.ds(pl.multiple_of((back - d) * grp + b * tok, tok), tok)
        ref = kvbuf.at[0, which, rows, :]
        pltpu.make_async_copy(ref, ref, kvr.at[d, b, which]).wait()

    odd_near = jnp.logical_and(k % 2 == 1, k + 2 < n_grp)
    relayed = jnp.logical_and(odd_near, a == G - 1)
    relays = jnp.logical_and(k % 2 == 1, k >= 3)

    def sends(d):
        near = k + d < n_grp
        if d == 1 and back >= 2:
            near = jnp.logical_and(near, jnp.logical_not(relayed))
        return near

    def relay_copy(b, which):
        src = pl.ds(pl.multiple_of((back - 2) * grp + b * tok, tok), tok)
        dst = pl.ds(pl.multiple_of((back - 1) * grp + b * tok, tok), tok)
        return pltpu.make_async_remote_copy(
            src_ref=kvbuf.at[0, which, src, :], dst_ref=kvbuf.at[0, which, dst, :],
            send_sem=fwd.at[b, which], recv_sem=kvr.at[1, b, which],
            device_id=(srv - G, z), device_id_type=MESH)

    def start_kv(d, when):
        @pl.when(jnp.logical_and(sends(d), when))
        def _():
            pairs = [(i, which) for which in range(2) for i in range(G)]
            for i, which in pairs if d == 1 else sorted(pairs):
                kv_copy(d, i, which).start()

    moved = pl.ds((G - 1) * kw, kw)

    def cross_kv(which):
        src = ksend.at[:, moved] if which == 0 else kvin.at[1, :, moved]
        return pltpu.make_async_remote_copy(
            src_ref=src, dst_ref=fkv.at[which], send_sem=xs.at[which], recv_sem=xr.at[which],
            device_id=(srv, partner), device_id_type=MESH)

    def cross_q():
        there = nbm - 1 - mine_half
        src = pl.ds(pl.multiple_of(there * R, R), R)
        return pltpu.make_async_remote_copy(
            src_ref=q_ref.at[src, pl.ds((G - 1) * width, width)], dst_ref=qraw.at[a, mine_half],
            send_sem=xs.at[2], recv_sem=qr.at[a, mine_half],
            device_id=(k * G + G - 1, partner), device_id_type=MESH)

    def chip_q(i, p):
        b = (a + i) % G
        return pltpu.make_async_remote_copy(
            src_ref=q_ref.at[part_rows(p), cols_of(b)], dst_ref=qraw.at[a, p],
            send_sem=qs.at[i, p], recv_sem=qr.at[a, p],
            device_id=(k * G + b, z), device_id_type=MESH)

    def chip_kept(i, p):
        b = (a + i) % G
        away = jnp.logical_and(jnp.logical_and(serves, b == G - 1), mine_half != p)
        return jnp.logical_not(away)

    if swap:
        @pl.when(inner)
        def _():
            cross_kv(0).start()
            cross_kv(1).start()
            cross_q().start()
    if chain:
        say_in()
    for d in range(1, back + 1):
        start_kv(d, a == G - 1 if d == back else True)
    for i in range(1, G):
        for which in range(2):
            kv_copy(0, i, which).start()
        for p in range(nbm):
            @pl.when(chip_kept(i, p))
            def _():
                chip_q(i, p).start()

    def q_wait(b, p):
        pltpu.make_async_copy(qraw.at[b, p], qraw.at[b, p], qr.at[b, p]).wait()

    def rotate_queries(b, p, part):
        rows = pl.ds(pl.multiple_of(part * R, R), R)
        cosine = table[b, 0, rows, :]
        sine = table[b, 1, rows, :]
        dst = pl.ds(pl.multiple_of((b * nbm + p) * R, R), R)
        for h in range(heads):
            qrot[h, dst, :] = rotate(qraw[b, p, :, h * HEAD:(h + 1) * HEAD], cosine, sine)

    def take_queries(b):
        for p in range(nbm):
            @pl.when(kept(p))
            def _():
                q_wait(b, p)
                rotate_queries(b, p, p)

    for d in range(1, back + 1):
        @pl.when(k - d < 0)
        def _():
            for sel in range(2 if swap else 1):
                kvbuf[sel, :, pl.ds((back - d) * grp, grp), :] = jnp.zeros((2, grp, kw), jnp.bfloat16)

    take_queries(a)
    for i in range(1, G):
        b = (a + i) % G
        make_table(b)
        take_queries(b)

    start_kv(back, a < G - 1)
    def pass_copy(d, which):
        rows = pl.ds(pl.multiple_of((back - d) * grp + a * tok, tok), tok)
        return pltpu.make_async_remote_copy(
            src_ref=fkv.at[which], dst_ref=kvbuf.at[1, which, rows, :],
            send_sem=fs.at[d, which], recv_sem=fr.at[d, a, which],
            device_id=((k + d) * G + G - 1, z), device_id_type=MESH)

    def passes(d):
        if d == 0:
            return a < G - 1
        near = k + d < n_grp
        if d == 1 and back >= 2:
            near = jnp.logical_and(near, jnp.logical_not(odd_near))
        return near

    hands_on = jnp.logical_and(relays, swapped)

    def hand_copy(b, which):
        src = pl.ds(pl.multiple_of((back - 2) * grp + b * tok, tok), tok)
        dst = pl.ds(pl.multiple_of((back - 1) * grp + b * tok, tok), tok)
        return pltpu.make_async_remote_copy(
            src_ref=kvbuf.at[1, which, src, :], dst_ref=kvbuf.at[1, which, dst, :],
            send_sem=hs.at[b, which], recv_sem=fr.at[1, b, which],
            device_id=(srv - G, z), device_id_type=MESH)

    def moved_wait(d, b, which):
        rows = pl.ds((back - d) * grp + b * tok, tok)
        ref = kvbuf.at[1, which, rows, :]
        pltpu.make_async_copy(ref, ref, fr.at[d, b, which]).wait()

    def pass_on(which):
        @pl.when(inner)
        def _():
            pltpu.make_async_copy(fkv.at[which], fkv.at[which], xr.at[which]).wait()
            for d in range(back, -1, -1):
                @pl.when(passes(d))
                def _():
                    pass_copy(d, which).start()

            @pl.when(swapped)
            def _():
                kvbuf[1, which, own_rows, :] = fkv[which]

    for which in range(2):
        if back >= 2:
            @pl.when(relays)
            def _():
                kv_wait(2, G - 1, which)
                relay_copy(G - 1, which).start()
        if swap:
            pass_on(which)

    def wait_moved():
        for which in range(2):
            for d in range(back + 1):
                for b in range(G):
                    if d == 0:
                        if b < G - 1:
                            moved_wait(d, b, which)
                    else:
                        ready = k - d >= 0
                        if d == 2:
                            ready = jnp.logical_and(ready, jnp.logical_not(relays))

                        @pl.when(ready)
                        def _():
                            moved_wait(d, b, which)

    def kv_wait_new(d, b, which):
        if (d, b) == (2, G - 1):
            @pl.when(jnp.logical_not(relays))
            def _():
                kv_wait(d, b, which)
        else:
            kv_wait(d, b, which)

    def wait_early(which):
        for i in range(1, G):
            kv_wait(0, (a + i) % G, which)
        for d in range(1, back + 1):
            @pl.when(k - d >= 0)
            def _():
                for b in range(G - 1 if d == back else 0, G):
                    kv_wait_new(d, b, which)

    def wait_late():
        @pl.when(k - back >= 0)
        def _():
            for b in range(G - 1):
                for which in range(2):
                    kv_wait_new(back, b, which)

    if chain:
        @pl.when(z == n_head // 2)
        def _():
            pl.semaphore_wait(far, 2)
            tell(z - 1)
            tell(z + 1)

        @pl.when(first_inner)
        def _():
            pl.semaphore_wait(far, 1)
            tell(0)

        @pl.when(z == 0)
        def _():
            pl.semaphore_wait(far, 2)

        @pl.when(z == n_head - 1)
        def _():
            pl.semaphore_wait(far, 1)

    wait_early(0)

    edge = n_head // 4
    outer = jnp.logical_or(z < edge, z >= n_head - edge)
    scale = HEAD ** -0.5 * math.log2(math.e)

    def pick(blk, order):
        out = jnp.int32(order[-1])
        for i in range(len(order) - 1):
            out = jnp.where(blk == i, order[i], out)
        return out

    def order_of(blk):
        if nblk != 4:
            return blk
        def both(i):
            return jnp.where(k == 0, pick(blk, ORDS[3 + i]), pick(blk, ORDS[i]))

        outer_blk = jnp.where(mine_half == 0, both(0), both(2))
        low = jnp.logical_and(jnp.logical_and(inner, mine_half == 0), a < G - 1)
        return jnp.where(outer, outer_blk, jnp.where(low, both(1), blk))

    def where_of(u):
        blk = u // nch
        c = u % nch
        blk = order_of(blk)
        b = jnp.where(k == 0, blk % G, G - 1 - blk % G)
        slot = (mine_half + jnp.where(swapped, 0, 1) + blk // G) % nbm
        foreign = jnp.where(jnp.logical_and(swapped, slot != mine_half), 1, 0)
        part = jnp.where(foreign == 1, mine_half, slot)
        return c, b, slot, part, foreign

    def make_bias(u):
        c, b, slot, part, foreign = where_of(u)
        r0 = pl.multiple_of(b * tok + part * R, R)
        rows = k * grp + r0 + lax.broadcasted_iota(jnp.int32, (R, HEAD), 0)
        start = starts_of(rows)
        for j in range(W // HEAD):
            t = (k - back) * grp + r0 + j * HEAD + lax.broadcasted_iota(jnp.int32, (R, HEAD), 1)
            ok = jnp.logical_and(t >= start, t <= rows)
            bias[:, j * HEAD:(j + 1) * HEAD] = jnp.where(ok, 0.0, -1e30)

    def scores(u, sc, mx):
        c, b, slot, part, foreign = where_of(u)
        r0 = pl.multiple_of(b * tok + part * R, R)
        q0 = pl.multiple_of((b * nbm + slot) * R, R)
        kcol = pl.ds(pl.multiple_of((c * chunk // per) * HEAD, HEAD), HEAD)
        q = qrot[pl.ds(c * chunk, chunk), pl.ds(q0, R), :].reshape(rows_u, HEAD)
        top = None
        for t0 in range(0, W, 2 * HEAD):
            n = min(2 * HEAD, W - t0)
            keys = kvbuf[foreign, 0, pl.ds(pl.multiple_of(r0 + t0, HEAD), n), kcol]
            s = lax.dot_general(q, keys, (((1,), (1,)), ((), ())), preferred_element_type=jnp.float32)
            s = (s.reshape(chunk, R, n) + bias[:, t0:t0 + n][None]).reshape(rows_u, n)
            sc[:, t0:t0 + n] = s
            m = functools.reduce(jnp.maximum, [s[:, h:h + HEAD] for h in range(0, n, HEAD)])
            top = m if top is None else jnp.maximum(top, m)
        mx[...] = jnp.broadcast_to(jnp.max(top, axis=1, keepdims=True), (rows_u, HEAD))

    def attend(u, sc, mx):
        c, b, slot, part, foreign = where_of(u)
        r0 = pl.multiple_of(b * tok + part * R, R)
        kcol = pl.ds(pl.multiple_of((c * chunk // per) * HEAD, HEAD), HEAD)
        top = mx[...]
        acc = None
        for t0 in range(0, W, 2 * HEAD):
            n = min(2 * HEAD, W - t0)
            peak = jnp.concatenate([top] * (n // HEAD), axis=1)
            w = jnp.exp2((sc[:, t0:t0 + n] - peak) * scale).astype(jnp.bfloat16)
            vals = kvbuf[foreign, 1, pl.ds(pl.multiple_of(r0 + t0, HEAD), n), kcol]
            vals = jnp.concatenate([vals, jnp.ones_like(vals)], axis=1)
            part_acc = lax.dot_general(w, vals, (((1,), (0,)), ((), ())), preferred_element_type=jnp.float32)
            acc = part_acc if acc is None else acc + part_acc
        o = (acc[:, :HEAD] / acc[:, HEAD:]).astype(jnp.bfloat16)
        for h in range(chunk):
            obuf[u, :, h * HEAD:(h + 1) * HEAD] = o[h * R:(h + 1) * R, :]

    def out_copy(u, j):
        c, b, slot, part, foreign = where_of(u)
        dest = part * per_blk + j
        zsrc = jnp.where(foreign == 1, partner, z)
        col = pl.multiple_of(zsrc * (G * width) + a * width + c * cw, HEAD)
        src = obuf.at[u, pl.ds(j * T, T), :]
        dst = out_ref.at[:, pl.ds(col, cw)]
        remote = pltpu.make_async_remote_copy(
            src_ref=src, dst_ref=dst, send_sem=osend.at[u * per_blk + j], recv_sem=orecv.at[0],
            device_id=(k * G + b, dest), device_id_type=MESH)
        local = pltpu.make_async_copy(src, dst, orecv.at[0])
        mine = jnp.logical_and(b == a, dest == z)
        return mine, remote, local

    def held(u, j):
        if j < per_blk - 1 or nblk != 4 or per_blk < 2:
            return u < 0
        c, b, slot, part, foreign = where_of(u)
        plain = jnp.logical_not(swapped)
        return jnp.logical_and(jnp.logical_and(plain, u >= jnp.where(k == 0, nch // 2, 2 * nch)), jnp.logical_and(mine_half == 1, part == 0))

    def send_out(u):
        for j in range(per_blk):
            mine, remote, local = out_copy(u, j)

            @pl.when(mine)
            def _():
                local.start()

            @pl.when(jnp.logical_not(jnp.logical_or(mine, held(u, j))))
            def _():
                remote.start()

    def send_held(i, carry):
        u = i

        @pl.when(held(u, per_blk - 1))
        def _():
            out_copy(u, per_blk - 1)[1].start()
        return carry

    def open_block(u):
        blk = u // nch

        @pl.when(blk == 1)
        def _():
            wait_late()

        if swap:
            @pl.when(jnp.logical_and(swapped, blk == nblk // nbm))
            def _():
                wait_moved()
                for b in range(G):
                    q_wait(b, nbm - 1 - mine_half)
                    rotate_queries(b, nbm - 1 - mine_half, mine_half)

        make_bias(u)

    make_bias(0)
    scores(0, sc0, mx0)
    wait_early(1)

    def one_step(u, carry):
        if swap and back >= 2:
            @pl.when(jnp.logical_and(hands_on, u == nch // 2))
            def _():
                for which in range(2):
                    for b in range(G):
                        moved_wait(2, b, which)
                        hand_copy(b, which).start()

        @pl.when(jnp.logical_and((u + 1) % nch == 0, u + 1 < units))
        def _():
            open_block(u + 1)

        attend(u, sc0, mx0)
        scores(jnp.minimum(u + 1, units - 1), sc0, mx0)
        send_out(u)
        return carry

    lax.fori_loop(0, units, one_step, 0)
    lax.fori_loop(0, units, send_held, 0)

    for i in range(1, G):
        for which in (1, 0):
            kv_copy(0, i, which).wait_send()
        for p in range(nbm):
            @pl.when(chip_kept(i, p))
            def _():
                chip_q(i, p).wait_send()
    for d in range(1, back + 1):
        @pl.when(sends(d))
        def _():
            for i in range(G):
                for which in (1, 0):
                    kv_copy(d, i, which).wait_send()
    if back >= 2:
        @pl.when(relays)
        def _():
            for which in range(2):
                relay_copy(G - 1, which).wait_send()
    if swap:
        @pl.when(inner)
        def _():
            if back >= 2:
                @pl.when(hands_on)
                def _():
                    for which in range(2):
                        for b in range(G):
                            hand_copy(b, which).wait_send()

            @pl.when(serves)
            def _():
                cross_q().wait_send()

            for which in range(2):
                cross_kv(which).wait_send()
                for d in range(back + 1):
                    @pl.when(passes(d))
                    def _():
                        pass_copy(d, which).wait_send()

    def end_send(u, carry):
        for j in range(per_blk):
            mine, remote, local = out_copy(u, j)

            @pl.when(jnp.logical_not(mine))
            def _():
                remote.wait_send()
        return carry

    lax.fori_loop(0, units, end_send, 0)

    pltpu.make_async_copy(out_ref, out_ref, orecv.at[0]).wait()


def solution(mesh):
    n_srv, n_head = mesh.shape["srv"], mesh.shape["head"]

    def body(queries, key_value_pair, lengths):
        tok, qw = queries.shape
        kv_all = key_value_pair.shape[2] // HEAD
        G = 2 if kv_all % 2 == 0 and n_srv % 2 == 0 else 1
        kvh = kv_all // G
        per = qw // HEAD // kv_all
        grp = G * tok
        n_grp = n_srv // G
        back = n_grp // 2
        T = tok // n_head
        R = max(tok // 2, T)
        chunk = per // 4
        ndoc = lengths.shape[0]
        heads = kvh * per
        nch = heads // chunk
        units = (grp // R) * nch
        W = back * grp + R
        swap = True and G == 2 and n_head % 2 == 0 and tok // R == 2
        cfg = (n_srv, n_head, G, back, tok, kvh, per, R, chunk, ndoc, swap)
        bf = jnp.bfloat16
        dma = pltpu.SemaphoreType.DMA
        return pl.pallas_call(
            functools.partial(kernel, cfg),
            out_shape=pltpu.VMEM((T, qw * n_head), bf),
            in_specs=[
                pl.BlockSpec(memory_space=pltpu.SMEM),
                pl.BlockSpec(memory_space=pl.ANY),
                pl.BlockSpec(memory_space=pl.ANY),
            ],
            out_specs=pl.BlockSpec(memory_space=pl.ANY),
            scratch_shapes=[
                pltpu.VMEM((G, tok // R, R, heads * HEAD), bf),
                pltpu.VMEM((heads, grp, HEAD), bf),
                pltpu.VMEM((2, 2, (back + 1) * grp, kvh * HEAD), bf),
                pltpu.VMEM((2, tok, kv_all * HEAD), bf),
                pltpu.VMEM((tok, kv_all * HEAD), bf),
                pltpu.VMEM((2, tok, kvh * HEAD), bf),
                pltpu.VMEM((G, 2, tok, HEAD), jnp.float32),
                pltpu.VMEM((R, W), jnp.float32),
                pltpu.VMEM((chunk * R, W), jnp.float32),
                pltpu.VMEM((chunk * R, HEAD), jnp.float32),
                pltpu.VMEM((units, R, chunk * HEAD), bf),
                dma((1,)),
                dma((G, tok // R)),
                dma((G, tok // R)),
                dma((back + 1, G, 2)),
                dma((back + 1, G, 2)),
                dma((G, 2)),
                dma((3,)),
                dma((2,)),
                dma((back + 1, 2)),
                dma((back + 1, G, 2)),
                dma((G, 2)),
                pltpu.SemaphoreType.REGULAR,
                dma((units * (R // T),)),
                dma((1,)),
            ],
            compiler_params=pltpu.CompilerParams(collective_id=0, has_side_effects=True),
            name="attend",
        )(lengths, queries, key_value_pair)

    in_specs = (P("srv", "head"), P(None, "srv", "head"), P())
    out_specs = P(("srv", "head"), None)
    return jax.shard_map(body, mesh=mesh, in_specs=in_specs, out_specs=out_specs, check_vma=False)
```

```python
import functools
import math

import jax
import jax.numpy as jnp
from jax import lax
from jax.experimental import pallas as pl
from jax.experimental.pallas import tpu as pltpu
from jax.sharding import PartitionSpec as P

HEAD = 128
ORDS = ((0, 2, 3, 1), (2, 0, 1, 3), (0, 2, 3, 1), (0, 2, 3, 1), (2, 3, 0, 1), (0, 2, 3, 1))
MESH = pl.DeviceIdType.MESH


def kernel(cfg, len_ref, q_ref, kv_ref, out_ref, qraw, qrot, kvbuf, kvin, ksend, fkv, table, bias,
           sc0, mx0, obuf, lsem, qs, qr, kvs, kvr, fwd, xs, xr, fs, fr, hs, far, osend, orecv):
    n_srv, n_head, G, back, tok, kvh, per, R, chunk, ndoc, swap = cfg
    heads = kvh * per
    grp = G * tok
    n_grp = n_srv // G
    T = tok // n_head
    longest = back * grp
    W = longest + R
    width = heads * HEAD
    kw = kvh * HEAD
    nbm = tok // R
    nblk = grp // R
    nch = heads // chunk
    units = nblk * nch
    per_blk = R // T
    cw = chunk * HEAD
    rows_u = chunk * R
    srv = lax.axis_index("srv")
    z = lax.axis_index("head")
    k = srv // G
    a = srv % G

    mine_half = z // (n_head // nbm)
    partner = n_head - 1 - z
    if swap:
        inner = jnp.logical_or(z == n_head // 2 - 1, z == n_head // 2)
    else:
        inner = z < 0
    serves = inner
    swapped = jnp.logical_and(serves, a == G - 1)

    bar = pltpu.get_barrier_semaphore()

    own_kv = [pltpu.make_async_copy(kv_ref.at[i], kvin.at[i], lsem.at[i]) for i in range(2)]
    for c in own_kv:
        c.start()

    def cols_of(b):
        return pl.ds(pl.multiple_of(b * width, HEAD), width)

    def part_rows(p):
        return slice(p * R, (p + 1) * R)

    def own_q(p):
        return pltpu.make_async_copy(q_ref.at[part_rows(p), cols_of(a)], qraw.at[a, p], qr.at[a, p])

    def kept(p):
        return jnp.logical_not(jnp.logical_and(swapped, mine_half != p))

    for p in range(nbm):
        @pl.when(kept(p))
        def _():
            own_q(p).start()

    def greet(s, h):
        pl.semaphore_signal(bar, inc=1, device_id=(s, h), device_id_type=MESH)

    chain = swap and n_head == 4
    outward = jnp.where(mine_half == 0, 0, n_head - 1)
    first_inner = z == n_head // 2 - 1
    if chain:
        for b in range(G):
            @pl.when(z < n_head - 1)
            def _():
                greet(k * G + b, z + 1)

            @pl.when(z == n_head // 2)
            def _():
                greet(k * G + b, z - 1)
    else:
        for i in range(1, n_head):
            for b in range(G):
                greet(k * G + b, (z + i) % n_head)
    for i in range(1, G):
        greet(k * G + (a + i) % G, z)
    for d in range(1, back + 1):
        @pl.when(k + d < n_grp)
        def _():
            for b in range(G):
                greet((k + d) * G + b, z)

        @pl.when(k - d >= 0)
        def _():
            for b in range(G):
                greet((k - d) * G + b, z)

    ends = []
    total = jnp.int32(0)
    for i in range(ndoc):
        total = total + len_ref[i]
        ends.append(total)

    lane = lax.broadcasted_iota(jnp.int32, (tok, HEAD), 1)
    low = lane < HEAD // 2
    step_up = jnp.where(low, lane, lane - HEAD // 2).astype(jnp.float32) * (2.0 / HEAD)
    inverse = jnp.exp(-step_up * math.log(500000.0))

    def starts_of(rows):
        start = jnp.zeros_like(rows)
        for e in ends:
            start = jnp.where(e <= rows, e, start)
        return start

    def cos_sin(angle):
        turns = jnp.floor(angle * (2.0 / math.pi) + 0.5)
        r = ((angle - turns * 1.5703125) - turns * 4.837512969970703125e-4) - turns * 7.549789948768648e-8
        r2 = r * r
        s = r + r * r2 * (-1.6666654611e-1 + r2 * (8.3321608736e-3 - r2 * 1.9515295891e-4))
        c = 1.0 - 0.5 * r2 + r2 * r2 * (
            4.166664568298827e-2 + r2 * (-1.388731625493765e-3 + r2 * 2.443315711809948e-5))
        quarter = turns.astype(jnp.int32)
        odd = (quarter & 1) == 1
        sine = jnp.where(odd, c, s)
        cosine = jnp.where(odd, s, c)
        sine = jnp.where((quarter & 2) == 2, -sine, sine)
        cosine = jnp.where(((quarter + 1) & 2) == 2, -cosine, cosine)
        return cosine, sine

    def make_table(b):
        rows = (k * G + b) * tok + lax.broadcasted_iota(jnp.int32, (tok, HEAD), 0)
        angle = (rows - starts_of(rows)).astype(jnp.float32) * inverse
        cosine, sine = cos_sin(angle)
        table[b, 0] = cosine
        table[b, 1] = jnp.where(low, -sine, sine)

    def rotate(x, cosine, sine):
        x = x.astype(jnp.float32)
        return (x * cosine + pltpu.roll(x, HEAD // 2, 1) * sine).astype(jnp.bfloat16)

    make_table(a)
    own_kv[0].wait()
    for h in range(G * kvh):
        cols = slice(h * HEAD, (h + 1) * HEAD)
        ksend[:, cols] = rotate(kvin[0, :, cols], table[a, 0], table[a, 1])

    own_rows = pl.ds(pl.multiple_of(back * grp + a * tok, tok), tok)
    kv_cols = pl.ds(pl.multiple_of(a * kw, HEAD), kw)
    own_kv[1].wait()

    if chain:
        count = jnp.where(first_inner, 2, jnp.where(z == 0, 0, 1)) * G + (G - 1)
    else:
        count = (n_head - 1) * G + (G - 1)
    for d in range(1, back + 1):
        count = count + G * jnp.where(k + d < n_grp, 1, 0) + G * jnp.where(k - d >= 0, 1, 0)
    pl.semaphore_wait(bar, count)

    def tell(h):
        pl.semaphore_signal(far, inc=1, device_id=(srv, h), device_id_type=MESH)

    def say_in():
        @pl.when(first_inner)
        def _():
            tell(0)
            tell(z + 1)

        @pl.when(z == n_head - 1)
        def _():
            tell(z - 1)

    def kv_copy(d, i, which):
        b = (a + i) % G
        cols = pl.ds(pl.multiple_of(b * kw, HEAD), kw)
        src = ksend.at[:, cols] if which == 0 else kvin.at[1, :, cols]
        rows = pl.ds(pl.multiple_of((back - d) * grp + a * tok, tok), tok)
        return pltpu.make_async_remote_copy(
            src_ref=src, dst_ref=kvbuf.at[0, which, rows, :],
            send_sem=kvs.at[d, i, which], recv_sem=kvr.at[d, a, which],
            device_id=((k + d) * G + b, z), device_id_type=MESH)

    def kv_wait(d, b, which):
        rows = pl.ds(pl.multiple_of((back - d) * grp + b * tok, tok), tok)
        ref = kvbuf.at[0, which, rows, :]
        pltpu.make_async_copy(ref, ref, kvr.at[d, b, which]).wait()

    odd_near = jnp.logical_and(k % 2 == 1, k + 2 < n_grp)
    relayed = jnp.logical_and(odd_near, a == G - 1)
    relays = jnp.logical_and(k % 2 == 1, k >= 3)

    def sends(d):
        near = k + d < n_grp
        if d == 1 and back >= 2:
            near = jnp.logical_and(near, jnp.logical_not(relayed))
        return near

    def relay_copy(b, which):
        src = pl.ds(pl.multiple_of((back - 2) * grp + b * tok, tok), tok)
        dst = pl.ds(pl.multiple_of((back - 1) * grp + b * tok, tok), tok)
        return pltpu.make_async_remote_copy(
            src_ref=kvbuf.at[0, which, src, :], dst_ref=kvbuf.at[0, which, dst, :],
            send_sem=fwd.at[b, which], recv_sem=kvr.at[1, b, which],
            device_id=(srv - G, z), device_id_type=MESH)

    def start_kv(d, when):
        @pl.when(jnp.logical_and(sends(d), when))
        def _():
            pairs = [(i, which) for which in range(2) for i in range(G)]
            for i, which in pairs if d == 1 else sorted(pairs):
                kv_copy(d, i, which).start()

    moved = pl.ds((G - 1) * kw, kw)

    def cross_kv(which):
        src = ksend.at[:, moved] if which == 0 else kvin.at[1, :, moved]
        return pltpu.make_async_remote_copy(
            src_ref=src, dst_ref=fkv.at[which], send_sem=xs.at[which], recv_sem=xr.at[which],
            device_id=(srv, partner), device_id_type=MESH)

    def cross_q():
        there = nbm - 1 - mine_half
        src = pl.ds(pl.multiple_of(there * R, R), R)
        return pltpu.make_async_remote_copy(
            src_ref=q_ref.at[src, pl.ds((G - 1) * width, width)], dst_ref=qraw.at[a, mine_half],
            send_sem=xs.at[2], recv_sem=qr.at[a, mine_half],
            device_id=(k * G + G - 1, partner), device_id_type=MESH)

    def chip_q(i, p):
        b = (a + i) % G
        return pltpu.make_async_remote_copy(
            src_ref=q_ref.at[part_rows(p), cols_of(b)], dst_ref=qraw.at[a, p],
            send_sem=qs.at[i, p], recv_sem=qr.at[a, p],
            device_id=(k * G + b, z), device_id_type=MESH)

    def chip_kept(i, p):
        b = (a + i) % G
        away = jnp.logical_and(jnp.logical_and(serves, b == G - 1), mine_half != p)
        return jnp.logical_not(away)

    if swap:
        @pl.when(inner)
        def _():
            cross_kv(0).start()
            cross_kv(1).start()
            cross_q().start()
    if chain:
        say_in()
    for d in range(1, back + 1):
        start_kv(d, a == G - 1 if d == back else True)
    for i in range(1, G):
        for which in range(2):
            kv_copy(0, i, which).start()
        for p in range(nbm):
            @pl.when(chip_kept(i, p))
            def _():
                chip_q(i, p).start()

    def q_wait(b, p):
        pltpu.make_async_copy(qraw.at[b, p], qraw.at[b, p], qr.at[b, p]).wait()

    def rotate_queries(b, p, part):
        rows = pl.ds(pl.multiple_of(part * R, R), R)
        cosine = table[b, 0, rows, :]
        sine = table[b, 1, rows, :]
        dst = pl.ds(pl.multiple_of((b * nbm + p) * R, R), R)
        for h in range(heads):
            qrot[h, dst, :] = rotate(qraw[b, p, :, h * HEAD:(h + 1) * HEAD], cosine, sine)

    def take_queries(b):
        for p in range(nbm):
            @pl.when(kept(p))
            def _():
                q_wait(b, p)
                rotate_queries(b, p, p)

    for d in range(1, back + 1):
        @pl.when(k - d < 0)
        def _():
            for sel in range(2 if swap else 1):
                kvbuf[sel, :, pl.ds((back - d) * grp, grp), :] = jnp.zeros((2, grp, kw), jnp.bfloat16)

    kvbuf[0, 0, own_rows, :] = ksend[:, kv_cols]
    kvbuf[0, 1, own_rows, :] = kvin[1, :, kv_cols]
    take_queries(a)
    for i in range(1, G):
        b = (a + i) % G
        make_table(b)
        take_queries(b)

    start_kv(back, a < G - 1)
    def pass_copy(d, which):
        rows = pl.ds(pl.multiple_of((back - d) * grp + a * tok, tok), tok)
        return pltpu.make_async_remote_copy(
            src_ref=fkv.at[which], dst_ref=kvbuf.at[1, which, rows, :],
            send_sem=fs.at[d, which], recv_sem=fr.at[d, a, which],
            device_id=((k + d) * G + G - 1, z), device_id_type=MESH)

    def passes(d):
        if d == 0:
            return a < G - 1
        near = k + d < n_grp
        if d == 1 and back >= 2:
            near = jnp.logical_and(near, jnp.logical_not(odd_near))
        return near

    hands_on = jnp.logical_and(relays, swapped)

    def hand_copy(b, which):
        src = pl.ds(pl.multiple_of((back - 2) * grp + b * tok, tok), tok)
        dst = pl.ds(pl.multiple_of((back - 1) * grp + b * tok, tok), tok)
        return pltpu.make_async_remote_copy(
            src_ref=kvbuf.at[1, which, src, :], dst_ref=kvbuf.at[1, which, dst, :],
            send_sem=hs.at[b, which], recv_sem=fr.at[1, b, which],
            device_id=(srv - G, z), device_id_type=MESH)

    def moved_wait(d, b, which):
        rows = pl.ds((back - d) * grp + b * tok, tok)
        ref = kvbuf.at[1, which, rows, :]
        pltpu.make_async_copy(ref, ref, fr.at[d, b, which]).wait()

    def pass_on(which):
        @pl.when(inner)
        def _():
            pltpu.make_async_copy(fkv.at[which], fkv.at[which], xr.at[which]).wait()
            for d in range(back, -1, -1):
                @pl.when(passes(d))
                def _():
                    pass_copy(d, which).start()

            @pl.when(swapped)
            def _():
                kvbuf[1, which, own_rows, :] = fkv[which]

    for which in range(2):
        if back >= 2:
            @pl.when(relays)
            def _():
                kv_wait(2, G - 1, which)
                relay_copy(G - 1, which).start()
        if swap:
            pass_on(which)

    def wait_moved():
        for which in range(2):
            for d in range(back + 1):
                for b in range(G):
                    if d == 0:
                        if b < G - 1:
                            moved_wait(d, b, which)
                    else:
                        ready = k - d >= 0
                        if d == 2:
                            ready = jnp.logical_and(ready, jnp.logical_not(relays))

                        @pl.when(ready)
                        def _():
                            moved_wait(d, b, which)

    def kv_wait_new(d, b, which):
        if (d, b) == (2, G - 1):
            @pl.when(jnp.logical_not(relays))
            def _():
                kv_wait(d, b, which)
        else:
            kv_wait(d, b, which)

    def wait_early(which):
        for i in range(1, G):
            kv_wait(0, (a + i) % G, which)
        for d in range(1, back + 1):
            @pl.when(k - d >= 0)
            def _():
                for b in range(G - 1 if d == back else 0, G):
                    kv_wait_new(d, b, which)

    def wait_late():
        @pl.when(k - back >= 0)
        def _():
            for b in range(G - 1):
                for which in range(2):
                    kv_wait_new(back, b, which)

    if chain:
        @pl.when(z == n_head // 2)
        def _():
            pl.semaphore_wait(far, 2)
            tell(z - 1)
            tell(z + 1)

        @pl.when(first_inner)
        def _():
            pl.semaphore_wait(far, 1)
            tell(0)

        @pl.when(z == 0)
        def _():
            pl.semaphore_wait(far, 2)

        @pl.when(z == n_head - 1)
        def _():
            pl.semaphore_wait(far, 1)

    wait_early(0)

    edge = n_head // 4
    outer = jnp.logical_or(z < edge, z >= n_head - edge)
    scale = HEAD ** -0.5 * math.log2(math.e)

    def pick(blk, order):
        out = jnp.int32(order[-1])
        for i in range(len(order) - 1):
            out = jnp.where(blk == i, order[i], out)
        return out

    def order_of(blk):
        if nblk != 4:
            return blk
        def both(i):
            return jnp.where(k == 0, pick(blk, ORDS[3 + i]), pick(blk, ORDS[i]))

        outer_blk = jnp.where(mine_half == 0, both(0), both(2))
        low = jnp.logical_and(jnp.logical_and(inner, mine_half == 0), a < G - 1)
        return jnp.where(outer, outer_blk, jnp.where(low, both(1), blk))

    def where_of(u):
        blk = u // nch
        c = u % nch
        blk = order_of(blk)
        b = jnp.where(k == 0, blk % G, G - 1 - blk % G)
        slot = (mine_half + jnp.where(swapped, 0, 1) + blk // G) % nbm
        foreign = jnp.where(jnp.logical_and(swapped, slot != mine_half), 1, 0)
        part = jnp.where(foreign == 1, mine_half, slot)
        return c, b, slot, part, foreign

    def make_bias(u):
        c, b, slot, part, foreign = where_of(u)
        r0 = pl.multiple_of(b * tok + part * R, R)
        rows = k * grp + r0 + lax.broadcasted_iota(jnp.int32, (R, HEAD), 0)
        start = starts_of(rows)
        for j in range(W // HEAD):
            t = (k - back) * grp + r0 + j * HEAD + lax.broadcasted_iota(jnp.int32, (R, HEAD), 1)
            ok = jnp.logical_and(t >= start, t <= rows)
            bias[:, j * HEAD:(j + 1) * HEAD] = jnp.where(ok, 0.0, -1e30)

    def scores(u, sc, mx):
        c, b, slot, part, foreign = where_of(u)
        r0 = pl.multiple_of(b * tok + part * R, R)
        q0 = pl.multiple_of((b * nbm + slot) * R, R)
        kcol = pl.ds(pl.multiple_of((c * chunk // per) * HEAD, HEAD), HEAD)
        q = qrot[pl.ds(c * chunk, chunk), pl.ds(q0, R), :].reshape(rows_u, HEAD)
        top = None
        for t0 in range(0, W, 2 * HEAD):
            n = min(2 * HEAD, W - t0)
            keys = kvbuf[foreign, 0, pl.ds(pl.multiple_of(r0 + t0, HEAD), n), kcol]
            s = lax.dot_general(q, keys, (((1,), (1,)), ((), ())), preferred_element_type=jnp.float32)
            s = (s.reshape(chunk, R, n) + bias[:, t0:t0 + n][None]).reshape(rows_u, n)
            sc[:, t0:t0 + n] = s
            m = functools.reduce(jnp.maximum, [s[:, h:h + HEAD] for h in range(0, n, HEAD)])
            top = m if top is None else jnp.maximum(top, m)
        mx[...] = jnp.broadcast_to(jnp.max(top, axis=1, keepdims=True), (rows_u, HEAD))

    def attend(u, sc, mx):
        c, b, slot, part, foreign = where_of(u)
        r0 = pl.multiple_of(b * tok + part * R, R)
        kcol = pl.ds(pl.multiple_of((c * chunk // per) * HEAD, HEAD), HEAD)
        top = mx[...]
        acc = None
        for t0 in range(0, W, 2 * HEAD):
            n = min(2 * HEAD, W - t0)
            peak = jnp.concatenate([top] * (n // HEAD), axis=1)
            w = jnp.exp2((sc[:, t0:t0 + n] - peak) * scale).astype(jnp.bfloat16)
            vals = kvbuf[foreign, 1, pl.ds(pl.multiple_of(r0 + t0, HEAD), n), kcol]
            vals = jnp.concatenate([vals, jnp.ones_like(vals)], axis=1)
            part_acc = lax.dot_general(w, vals, (((1,), (0,)), ((), ())), preferred_element_type=jnp.float32)
            acc = part_acc if acc is None else acc + part_acc
        o = (acc[:, :HEAD] / acc[:, HEAD:]).astype(jnp.bfloat16)
        for h in range(chunk):
            obuf[u, :, h * HEAD:(h + 1) * HEAD] = o[h * R:(h + 1) * R, :]

    def out_copy(u, j):
        c, b, slot, part, foreign = where_of(u)
        dest = part * per_blk + j
        zsrc = jnp.where(foreign == 1, partner, z)
        col = pl.multiple_of(zsrc * (G * width) + a * width + c * cw, HEAD)
        src = obuf.at[u, pl.ds(j * T, T), :]
        dst = out_ref.at[:, pl.ds(col, cw)]
        remote = pltpu.make_async_remote_copy(
            src_ref=src, dst_ref=dst, send_sem=osend.at[u * per_blk + j], recv_sem=orecv.at[0],
            device_id=(k * G + b, dest), device_id_type=MESH)
        local = pltpu.make_async_copy(src, dst, orecv.at[0])
        mine = jnp.logical_and(b == a, dest == z)
        return mine, remote, local

    def held(u, j):
        if j < per_blk - 1 or nblk != 4 or per_blk < 2:
            return u < 0
        c, b, slot, part, foreign = where_of(u)
        plain = jnp.logical_not(swapped)
        return jnp.logical_and(jnp.logical_and(plain, u >= jnp.where(k == 0, nch // 2, 2 * nch)), jnp.logical_and(mine_half == 1, part == 0))

    def send_out(u):
        for j in range(per_blk):
            mine, remote, local = out_copy(u, j)

            @pl.when(mine)
            def _():
                local.start()

            @pl.when(jnp.logical_not(jnp.logical_or(mine, held(u, j))))
            def _():
                remote.start()

    def send_held(i, carry):
        u = i

        @pl.when(held(u, per_blk - 1))
        def _():
            out_copy(u, per_blk - 1)[1].start()
        return carry

    def open_block(u):
        blk = u // nch

        @pl.when(blk == 1)
        def _():
            wait_late()

        if swap:
            @pl.when(jnp.logical_and(swapped, blk == nblk // nbm))
            def _():
                wait_moved()
                for b in range(G):
                    q_wait(b, nbm - 1 - mine_half)
                    rotate_queries(b, nbm - 1 - mine_half, mine_half)

        make_bias(u)

    make_bias(0)
    scores(0, sc0, mx0)
    wait_early(1)

    def one_step(u, carry):
        if swap and back >= 2:
            @pl.when(jnp.logical_and(hands_on, u == nch // 2))
            def _():
                for which in range(2):
                    for b in range(G):
                        moved_wait(2, b, which)
                        hand_copy(b, which).start()

        @pl.when(jnp.logical_and((u + 1) % nch == 0, u + 1 < units))
        def _():
            open_block(u + 1)

        attend(u, sc0, mx0)
        scores(jnp.minimum(u + 1, units - 1), sc0, mx0)
        send_out(u)
        return carry

    lax.fori_loop(0, units, one_step, 0)
    lax.fori_loop(0, units, send_held, 0)

    for i in range(1, G):
        for which in (1, 0):
            kv_copy(0, i, which).wait_send()
        for p in range(nbm):
            @pl.when(chip_kept(i, p))
            def _():
                chip_q(i, p).wait_send()
    for d in range(1, back + 1):
        @pl.when(sends(d))
        def _():
            for i in range(G):
                for which in (1, 0):
                    kv_copy(d, i, which).wait_send()
    if back >= 2:
        @pl.when(relays)
        def _():
            for which in range(2):
                relay_copy(G - 1, which).wait_send()
    if swap:
        @pl.when(inner)
        def _():
            if back >= 2:
                @pl.when(hands_on)
                def _():
                    for which in range(2):
                        for b in range(G):
                            hand_copy(b, which).wait_send()

            @pl.when(serves)
            def _():
                cross_q().wait_send()

            for which in range(2):
                cross_kv(which).wait_send()
                for d in range(back + 1):
                    @pl.when(passes(d))
                    def _():
                        pass_copy(d, which).wait_send()

    def end_send(u, carry):
        for j in range(per_blk):
            mine, remote, local = out_copy(u, j)

            @pl.when(jnp.logical_not(mine))
            def _():
                remote.wait_send()
        return carry

    lax.fori_loop(0, units, end_send, 0)

    pltpu.make_async_copy(out_ref, out_ref, orecv.at[0]).wait()


def solution(mesh):
    n_srv, n_head = mesh.shape["srv"], mesh.shape["head"]

    def body(queries, key_value_pair, lengths):
        tok, qw = queries.shape
        kv_all = key_value_pair.shape[2] // HEAD
        G = 2 if kv_all % 2 == 0 and n_srv % 2 == 0 else 1
        kvh = kv_all // G
        per = qw // HEAD // kv_all
        grp = G * tok
        n_grp = n_srv // G
        back = n_grp // 2
        T = tok // n_head
        R = max(tok // 2, T)
        chunk = per // 4
        ndoc = lengths.shape[0]
        heads = kvh * per
        nch = heads // chunk
        units = (grp // R) * nch
        W = back * grp + R
        swap = True and G == 2 and n_head % 2 == 0 and tok // R == 2
        cfg = (n_srv, n_head, G, back, tok, kvh, per, R, chunk, ndoc, swap)
        bf = jnp.bfloat16
        dma = pltpu.SemaphoreType.DMA
        return pl.pallas_call(
            functools.partial(kernel, cfg),
            out_shape=pltpu.VMEM((T, qw * n_head), bf),
            in_specs=[
                pl.BlockSpec(memory_space=pltpu.SMEM),
                pl.BlockSpec(memory_space=pl.ANY),
                pl.BlockSpec(memory_space=pl.ANY),
            ],
            out_specs=pl.BlockSpec(memory_space=pl.ANY),
            scratch_shapes=[
                pltpu.VMEM((G, tok // R, R, heads * HEAD), bf),
                pltpu.VMEM((heads, grp, HEAD), bf),
                pltpu.VMEM((2, 2, (back + 1) * grp, kvh * HEAD), bf),
                pltpu.VMEM((2, tok, kv_all * HEAD), bf),
                pltpu.VMEM((tok, kv_all * HEAD), bf),
                pltpu.VMEM((2, tok, kvh * HEAD), bf),
                pltpu.VMEM((G, 2, tok, HEAD), jnp.float32),
                pltpu.VMEM((R, W), jnp.float32),
                pltpu.VMEM((chunk * R, W), jnp.float32),
                pltpu.VMEM((chunk * R, HEAD), jnp.float32),
                pltpu.VMEM((units, R, chunk * HEAD), bf),
                dma((2,)),
                dma((G, tok // R)),
                dma((G, tok // R)),
                dma((back + 1, G, 2)),
                dma((back + 1, G, 2)),
                dma((G, 2)),
                dma((3,)),
                dma((2,)),
                dma((back + 1, 2)),
                dma((back + 1, G, 2)),
                dma((G, 2)),
                pltpu.SemaphoreType.REGULAR,
                dma((units * (R // T),)),
                dma((1,)),
            ],
            compiler_params=pltpu.CompilerParams(collective_id=0, has_side_effects=True),
            name="attend",
        )(lengths, queries, key_value_pair)

    in_specs = (P("srv", "head"), P(None, "srv", "head"), P())
    out_specs = P(("srv", "head"), None)
    return jax.shard_map(body, mesh=mesh, in_specs=in_specs, out_specs=out_specs, check_vma=False)
```

```python
import functools
import math

import jax
import jax.numpy as jnp
from jax import lax
from jax.experimental import pallas as pl
from jax.experimental.pallas import tpu as pltpu
from jax.sharding import PartitionSpec as P

HEAD = 128
ORDS = ((0, 2, 3, 1), (2, 0, 1, 3), (0, 2, 3, 1), (0, 2, 3, 1), (2, 3, 0, 1), (0, 2, 3, 1))
MESH = pl.DeviceIdType.MESH


def kernel(cfg, len_ref, q_ref, kv_ref, out_ref, qraw, qrot, kvbuf, kvin, ksend, fkv, table, bias,
           sc0, mx0, obuf, lsem, qs, qr, kvs, kvr, fwd, xs, xr, fs, fr, hs, far, osend, orecv):
    n_srv, n_head, G, back, tok, kvh, per, R, chunk, ndoc, swap = cfg
    heads = kvh * per
    grp = G * tok
    n_grp = n_srv // G
    T = tok // n_head
    longest = back * grp
    W = longest + R
    width = heads * HEAD
    kw = kvh * HEAD
    nbm = tok // R
    nblk = grp // R
    nch = heads // chunk
    units = nblk * nch
    per_blk = R // T
    cw = chunk * HEAD
    rows_u = chunk * R
    srv = lax.axis_index("srv")
    z = lax.axis_index("head")
    k = srv // G
    a = srv % G

    mine_half = z // (n_head // nbm)
    partner = n_head - 1 - z
    if swap:
        inner = jnp.logical_or(z == n_head // 2 - 1, z == n_head // 2)
    else:
        inner = z < 0
    serves = inner
    swapped = jnp.logical_and(serves, a == G - 1)

    bar = pltpu.get_barrier_semaphore()

    own_kv = [pltpu.make_async_copy(kv_ref.at[i], kvin.at[i], lsem.at[i]) for i in range(2)]
    for c in own_kv:
        c.start()

    def cols_of(b):
        return pl.ds(pl.multiple_of(b * width, HEAD), width)

    def part_rows(p):
        return slice(p * R, (p + 1) * R)

    def own_q(p):
        return pltpu.make_async_copy(q_ref.at[part_rows(p), cols_of(a)], qraw.at[a, p], qr.at[a, p])

    def kept(p):
        return jnp.logical_not(jnp.logical_and(swapped, mine_half != p))

    for p in range(nbm):
        @pl.when(kept(p))
        def _():
            own_q(p).start()

    def greet(s, h):
        pl.semaphore_signal(bar, inc=1, device_id=(s, h), device_id_type=MESH)

    chain = swap and n_head == 4
    outward = jnp.where(mine_half == 0, 0, n_head - 1)
    first_inner = z == n_head // 2 - 1
    if chain:
        for b in range(G):
            @pl.when(z < n_head - 1)
            def _():
                greet(k * G + b, z + 1)

            @pl.when(z == n_head // 2)
            def _():
                greet(k * G + b, z - 1)
    else:
        for i in range(1, n_head):
            for b in range(G):
                greet(k * G + b, (z + i) % n_head)
    for i in range(1, G):
        greet(k * G + (a + i) % G, z)
    for d in range(1, back + 1):
        @pl.when(k + d < n_grp)
        def _():
            for b in range(G):
                greet((k + d) * G + b, z)

        @pl.when(k - d >= 0)
        def _():
            for b in range(G):
                greet((k - d) * G + b, z)

    ends = []
    total = jnp.int32(0)
    for i in range(ndoc):
        total = total + len_ref[i]
        ends.append(total)

    lane = lax.broadcasted_iota(jnp.int32, (tok, HEAD), 1)
    low = lane < HEAD // 2
    step_up = jnp.where(low, lane, lane - HEAD // 2).astype(jnp.float32) * (2.0 / HEAD)
    inverse = jnp.exp(-step_up * math.log(500000.0))

    def starts_of(rows):
        start = jnp.zeros_like(rows)
        for e in ends:
            start = jnp.where(e <= rows, e, start)
        return start

    def cos_sin(angle):
        turns = jnp.floor(angle * (2.0 / math.pi) + 0.5)
        r = ((angle - turns * 1.5703125) - turns * 4.837512969970703125e-4) - turns * 7.549789948768648e-8
        r2 = r * r
        s = r + r * r2 * (-1.6666654611e-1 + r2 * (8.3321608736e-3 - r2 * 1.9515295891e-4))
        c = 1.0 - 0.5 * r2 + r2 * r2 * (
            4.166664568298827e-2 + r2 * (-1.388731625493765e-3 + r2 * 2.443315711809948e-5))
        quarter = turns.astype(jnp.int32)
        odd = (quarter & 1) == 1
        sine = jnp.where(odd, c, s)
        cosine = jnp.where(odd, s, c)
        sine = jnp.where((quarter & 2) == 2, -sine, sine)
        cosine = jnp.where(((quarter + 1) & 2) == 2, -cosine, cosine)
        return cosine, sine

    def make_table(b):
        rows = (k * G + b) * tok + lax.broadcasted_iota(jnp.int32, (tok, HEAD), 0)
        angle = (rows - starts_of(rows)).astype(jnp.float32) * inverse
        cosine, sine = cos_sin(angle)
        table[b, 0] = cosine
        table[b, 1] = jnp.where(low, -sine, sine)

    def rotate(x, cosine, sine):
        x = x.astype(jnp.float32)
        return (x * cosine + pltpu.roll(x, HEAD // 2, 1) * sine).astype(jnp.bfloat16)

    make_table(a)
    own_kv[0].wait()
    for h in range(G * kvh):
        cols = slice(h * HEAD, (h + 1) * HEAD)
        ksend[:, cols] = rotate(kvin[0, :, cols], table[a, 0], table[a, 1])

    own_rows = pl.ds(pl.multiple_of(back * grp + a * tok, tok), tok)
    kv_cols = pl.ds(pl.multiple_of(a * kw, HEAD), kw)
    own_kv[1].wait()

    if chain:
        count = jnp.where(first_inner, 2, jnp.where(z == 0, 0, 1)) * G + (G - 1)
    else:
        count = (n_head - 1) * G + (G - 1)
    for d in range(1, back + 1):
        count = count + G * jnp.where(k + d < n_grp, 1, 0) + G * jnp.where(k - d >= 0, 1, 0)
    pl.semaphore_wait(bar, count)

    def tell(h):
        pl.semaphore_signal(far, inc=1, device_id=(srv, h), device_id_type=MESH)

    def say_in():
        @pl.when(first_inner)
        def _():
            tell(0)
            tell(z + 1)

        @pl.when(z == n_head - 1)
        def _():
            tell(z - 1)

    def kv_copy(d, i, which):
        b = (a + i) % G
        cols = pl.ds(pl.multiple_of(b * kw, HEAD), kw)
        src = ksend.at[:, cols] if which == 0 else kvin.at[1, :, cols]
        rows = pl.ds(pl.multiple_of((back - d) * grp + a * tok, tok), tok)
        return pltpu.make_async_remote_copy(
            src_ref=src, dst_ref=kvbuf.at[0, which, rows, :],
            send_sem=kvs.at[d, i, which], recv_sem=kvr.at[d, a, which],
            device_id=((k + d) * G + b, z), device_id_type=MESH)

    def kv_wait(d, b, which):
        rows = pl.ds(pl.multiple_of((back - d) * grp + b * tok, tok), tok)
        ref = kvbuf.at[0, which, rows, :]
        pltpu.make_async_copy(ref, ref, kvr.at[d, b, which]).wait()

    odd_near = jnp.logical_and(k % 2 == 1, k + 2 < n_grp)
    relayed = jnp.logical_and(odd_near, a == G - 1)
    relays = jnp.logical_and(k % 2 == 1, k >= 3)

    def sends(d):
        near = k + d < n_grp
        if d == 1 and back >= 2:
            near = jnp.logical_and(near, jnp.logical_not(relayed))
        return near

    def relay_copy(b, which):
        src = pl.ds(pl.multiple_of((back - 2) * grp + b * tok, tok), tok)
        dst = pl.ds(pl.multiple_of((back - 1) * grp + b * tok, tok), tok)
        return pltpu.make_async_remote_copy(
            src_ref=kvbuf.at[0, which, src, :], dst_ref=kvbuf.at[0, which, dst, :],
            send_sem=fwd.at[b, which], recv_sem=kvr.at[1, b, which],
            device_id=(srv - G, z), device_id_type=MESH)

    def start_kv(d, when):
        @pl.when(jnp.logical_and(sends(d), when))
        def _():
            pairs = [(i, which) for which in range(2) for i in range(G)]
            for i, which in pairs if d == 1 else sorted(pairs):
                kv_copy(d, i, which).start()

    moved = pl.ds((G - 1) * kw, kw)

    def cross_kv(which):
        src = ksend.at[:, moved] if which == 0 else kvin.at[1, :, moved]
        return pltpu.make_async_remote_copy(
            src_ref=src, dst_ref=fkv.at[which], send_sem=xs.at[which], recv_sem=xr.at[which],
            device_id=(srv, partner), device_id_type=MESH)

    def cross_q():
        there = nbm - 1 - mine_half
        src = pl.ds(pl.multiple_of(there * R, R), R)
        return pltpu.make_async_remote_copy(
            src_ref=q_ref.at[src, pl.ds((G - 1) * width, width)], dst_ref=qraw.at[a, mine_half],
            send_sem=xs.at[2], recv_sem=qr.at[a, mine_half],
            device_id=(k * G + G - 1, partner), device_id_type=MESH)

    def chip_q(i, p):
        b = (a + i) % G
        return pltpu.make_async_remote_copy(
            src_ref=q_ref.at[part_rows(p), cols_of(b)], dst_ref=qraw.at[a, p],
            send_sem=qs.at[i, p], recv_sem=qr.at[a, p],
            device_id=(k * G + b, z), device_id_type=MESH)

    def chip_kept(i, p):
        b = (a + i) % G
        away = jnp.logical_and(jnp.logical_and(serves, b == G - 1), mine_half != p)
        return jnp.logical_not(away)

    if swap:
        @pl.when(inner)
        def _():
            cross_kv(0).start()
            cross_kv(1).start()
            cross_q().start()
    if chain:
        say_in()
    for d in range(1, back + 1):
        start_kv(d, a == G - 1 if d == back else True)
    for i in range(1, G):
        for which in range(2):
            kv_copy(0, i, which).start()
        for p in range(nbm):
            @pl.when(chip_kept(i, p))
            def _():
                chip_q(i, p).start()

    def q_wait(b, p):
        pltpu.make_async_copy(qraw.at[b, p], qraw.at[b, p], qr.at[b, p]).wait()

    def rotate_queries(b, p, part):
        rows = pl.ds(pl.multiple_of(part * R, R), R)
        cosine = table[b, 0, rows, :]
        sine = table[b, 1, rows, :]
        dst = pl.ds(pl.multiple_of((b * nbm + p) * R, R), R)
        for h in range(heads):
            qrot[h, dst, :] = rotate(qraw[b, p, :, h * HEAD:(h + 1) * HEAD], cosine, sine)

    def take_queries(b):
        for p in range(nbm):
            @pl.when(kept(p))
            def _():
                q_wait(b, p)
                rotate_queries(b, p, p)

    for d in range(1, back + 1):
        @pl.when(k - d < 0)
        def _():
            for sel in range(2 if swap else 1):
                kvbuf[sel, :, pl.ds((back - d) * grp, grp), :] = jnp.zeros((2, grp, kw), jnp.bfloat16)

    kvbuf[0, 0, own_rows, :] = ksend[:, kv_cols]
    kvbuf[0, 1, own_rows, :] = kvin[1, :, kv_cols]
    take_queries(a)
    for i in range(1, G):
        b = (a + i) % G
        make_table(b)
        take_queries(b)

    start_kv(back, a < G - 1)
    def pass_copy(d, which):
        rows = pl.ds(pl.multiple_of((back - d) * grp + a * tok, tok), tok)
        return pltpu.make_async_remote_copy(
            src_ref=fkv.at[which], dst_ref=kvbuf.at[1, which, rows, :],
            send_sem=fs.at[d, which], recv_sem=fr.at[d, a, which],
            device_id=((k + d) * G + G - 1, z), device_id_type=MESH)

    def passes(d):
        if d == 0:
            return a < G - 1
        near = k + d < n_grp
        if d == 1 and back >= 2:
            near = jnp.logical_and(near, jnp.logical_not(odd_near))
        return near

    hands_on = jnp.logical_and(relays, swapped)

    def hand_copy(b, which):
        src = pl.ds(pl.multiple_of((back - 2) * grp + b * tok, tok), tok)
        dst = pl.ds(pl.multiple_of((back - 1) * grp + b * tok, tok), tok)
        return pltpu.make_async_remote_copy(
            src_ref=kvbuf.at[1, which, src, :], dst_ref=kvbuf.at[1, which, dst, :],
            send_sem=hs.at[b, which], recv_sem=fr.at[1, b, which],
            device_id=(srv - G, z), device_id_type=MESH)

    def moved_wait(d, b, which):
        rows = pl.ds((back - d) * grp + b * tok, tok)
        ref = kvbuf.at[1, which, rows, :]
        pltpu.make_async_copy(ref, ref, fr.at[d, b, which]).wait()

    def pass_on(which):
        @pl.when(inner)
        def _():
            pltpu.make_async_copy(fkv.at[which], fkv.at[which], xr.at[which]).wait()
            for d in range(back, -1, -1):
                @pl.when(passes(d))
                def _():
                    pass_copy(d, which).start()

            @pl.when(swapped)
            def _():
                kvbuf[1, which, own_rows, :] = fkv[which]

    for which in range(2):
        if back >= 2:
            @pl.when(relays)
            def _():
                kv_wait(2, G - 1, which)
                relay_copy(G - 1, which).start()
        if swap:
            pass_on(which)

    def wait_moved():
        for which in range(2):
            for d in range(back + 1):
                for b in range(G):
                    if d == 0:
                        if b < G - 1:
                            moved_wait(d, b, which)
                    else:
                        ready = k - d >= 0
                        if d == 2:
                            ready = jnp.logical_and(ready, jnp.logical_not(relays))

                        @pl.when(ready)
                        def _():
                            moved_wait(d, b, which)

    def kv_wait_new(d, b, which):
        if (d, b) == (2, G - 1):
            @pl.when(jnp.logical_not(relays))
            def _():
                kv_wait(d, b, which)
        else:
            kv_wait(d, b, which)

    def wait_early(which):
        for i in range(1, G):
            kv_wait(0, (a + i) % G, which)
        for d in range(1, back + 1):
            @pl.when(k - d >= 0)
            def _():
                for b in range(G - 1 if d == back else 0, G):
                    kv_wait_new(d, b, which)

    def wait_late():
        @pl.when(k - back >= 0)
        def _():
            for b in range(G - 1):
                for which in range(2):
                    kv_wait_new(back, b, which)

    if chain:
        @pl.when(z == n_head // 2)
        def _():
            pl.semaphore_wait(far, 2)
            tell(z - 1)
            tell(z + 1)

        @pl.when(first_inner)
        def _():
            pl.semaphore_wait(far, 1)
            tell(0)

        @pl.when(z == 0)
        def _():
            pl.semaphore_wait(far, 2)

        @pl.when(z == n_head - 1)
        def _():
            pl.semaphore_wait(far, 1)

    wait_early(0)

    edge = n_head // 4
    outer = jnp.logical_or(z < edge, z >= n_head - edge)
    scale = HEAD ** -0.5 * math.log2(math.e)

    def pick(blk, order):
        out = jnp.int32(order[-1])
        for i in range(len(order) - 1):
            out = jnp.where(blk == i, order[i], out)
        return out

    def order_of(blk):
        if nblk != 4:
            return blk
        def both(i):
            return jnp.where(k == 0, pick(blk, ORDS[3 + i]), pick(blk, ORDS[i]))

        outer_blk = jnp.where(mine_half == 0, both(0), both(2))
        low = jnp.logical_and(jnp.logical_and(inner, mine_half == 0), a < G - 1)
        return jnp.where(outer, outer_blk, jnp.where(low, both(1), blk))

    def where_of(u):
        blk = u // nch
        c = u % nch
        blk = order_of(blk)
        b = jnp.where(k == 0, blk % G, G - 1 - blk % G)
        slot = (mine_half + jnp.where(swapped, 0, 1) + blk // G) % nbm
        foreign = jnp.where(jnp.logical_and(swapped, slot != mine_half), 1, 0)
        part = jnp.where(foreign == 1, mine_half, slot)
        return c, b, slot, part, foreign

    def make_bias(u):
        c, b, slot, part, foreign = where_of(u)
        r0 = pl.multiple_of(b * tok + part * R, R)
        rows = k * grp + r0 + lax.broadcasted_iota(jnp.int32, (R, HEAD), 0)
        start = starts_of(rows)
        for j in range(W // HEAD):
            t = (k - back) * grp + r0 + j * HEAD + lax.broadcasted_iota(jnp.int32, (R, HEAD), 1)
            ok = jnp.logical_and(t >= start, t <= rows)
            bias[:, j * HEAD:(j + 1) * HEAD] = jnp.where(ok, 0.0, -1e30)

    def scores(u, sc, mx):
        c, b, slot, part, foreign = where_of(u)
        r0 = pl.multiple_of(b * tok + part * R, R)
        q0 = pl.multiple_of((b * nbm + slot) * R, R)
        kcol = pl.ds(pl.multiple_of((c * chunk // per) * HEAD, HEAD), HEAD)
        q = qrot[pl.ds(c * chunk, chunk), pl.ds(q0, R), :].reshape(rows_u, HEAD)
        top = None
        for t0 in range(0, W, 2 * HEAD):
            n = min(2 * HEAD, W - t0)
            keys = kvbuf[foreign, 0, pl.ds(pl.multiple_of(r0 + t0, HEAD), n), kcol]
            s = lax.dot_general(q, keys, (((1,), (1,)), ((), ())), preferred_element_type=jnp.float32)
            s = (s.reshape(chunk, R, n) + bias[:, t0:t0 + n][None]).reshape(rows_u, n)
            sc[:, t0:t0 + n] = s
            m = functools.reduce(jnp.maximum, [s[:, h:h + HEAD] for h in range(0, n, HEAD)])
            top = m if top is None else jnp.maximum(top, m)
        mx[...] = jnp.broadcast_to(jnp.max(top, axis=1, keepdims=True), (rows_u, HEAD))

    def attend(u, sc, mx):
        c, b, slot, part, foreign = where_of(u)
        r0 = pl.multiple_of(b * tok + part * R, R)
        kcol = pl.ds(pl.multiple_of((c * chunk // per) * HEAD, HEAD), HEAD)
        top = mx[...]
        acc = None
        for t0 in range(0, W, 2 * HEAD):
            n = min(2 * HEAD, W - t0)
            peak = jnp.concatenate([top] * (n // HEAD), axis=1)
            w = jnp.exp2((sc[:, t0:t0 + n] - peak) * scale).astype(jnp.bfloat16)
            vals = kvbuf[foreign, 1, pl.ds(pl.multiple_of(r0 + t0, HEAD), n), kcol]
            vals = jnp.concatenate([vals, jnp.ones_like(vals)], axis=1)
            part_acc = lax.dot_general(w, vals, (((1,), (0,)), ((), ())), preferred_element_type=jnp.float32)
            acc = part_acc if acc is None else acc + part_acc
        o = (acc[:, :HEAD] / acc[:, HEAD:]).astype(jnp.bfloat16)
        for h in range(chunk):
            obuf[u, :, h * HEAD:(h + 1) * HEAD] = o[h * R:(h + 1) * R, :]

    def out_copy(u, j):
        c, b, slot, part, foreign = where_of(u)
        dest = part * per_blk + j
        zsrc = jnp.where(foreign == 1, partner, z)
        col = pl.multiple_of(zsrc * (G * width) + a * width + c * cw, HEAD)
        src = obuf.at[u, pl.ds(j * T, T), :]
        dst = out_ref.at[:, pl.ds(col, cw)]
        remote = pltpu.make_async_remote_copy(
            src_ref=src, dst_ref=dst, send_sem=osend.at[u * per_blk + j], recv_sem=orecv.at[0],
            device_id=(k * G + b, dest), device_id_type=MESH)
        local = pltpu.make_async_copy(src, dst, orecv.at[0])
        mine = jnp.logical_and(b == a, dest == z)
        return mine, remote, local

    def held(u, j):
        if j < per_blk - 1 or nblk != 4 or per_blk < 2:
            return u < 0
        c, b, slot, part, foreign = where_of(u)
        plain = jnp.logical_not(swapped)
        return jnp.logical_and(jnp.logical_and(plain, u >= jnp.where(k == 0, nch // 2, 2 * nch)), jnp.logical_and(mine_half == 1, part == 0))

    def send_out(u):
        for j in range(per_blk):
            mine, remote, local = out_copy(u, j)

            @pl.when(mine)
            def _():
                local.start()

            @pl.when(jnp.logical_not(jnp.logical_or(mine, held(u, j))))
            def _():
                remote.start()

    def send_held(i, carry):
        u = i

        @pl.when(held(u, per_blk - 1))
        def _():
            out_copy(u, per_blk - 1)[1].start()
        return carry

    def open_block(u):
        blk = u // nch

        @pl.when(blk == 1)
        def _():
            wait_late()

        if swap:
            @pl.when(jnp.logical_and(swapped, blk == nblk // nbm))
            def _():
                wait_moved()
                for b in range(G):
                    q_wait(b, nbm - 1 - mine_half)
                    rotate_queries(b, nbm - 1 - mine_half, mine_half)

        make_bias(u)

    make_bias(0)
    scores(0, sc0, mx0)
    wait_early(1)

    def one_step(u, carry):
        if swap and back >= 2:
            @pl.when(jnp.logical_and(hands_on, u == nch // 2))
            def _():
                for which in range(2):
                    for b in range(G):
                        moved_wait(2, b, which)
                        hand_copy(b, which).start()

        @pl.when(jnp.logical_and((u + 1) % nch == 0, u + 1 < units))
        def _():
            open_block(u + 1)

        attend(u, sc0, mx0)
        scores(jnp.minimum(u + 1, units - 1), sc0, mx0)
        send_out(u)
        return carry

    attend(0, sc0, mx0)
    send_out(0)
    scores(1, sc0, mx0)
    lax.fori_loop(1, units, one_step, 0)
    lax.fori_loop(0, units, send_held, 0)

    for i in range(1, G):
        for which in (1, 0):
            kv_copy(0, i, which).wait_send()
        for p in range(nbm):
            @pl.when(chip_kept(i, p))
            def _():
                chip_q(i, p).wait_send()
    for d in range(1, back + 1):
        @pl.when(sends(d))
        def _():
            for i in range(G):
                for which in (1, 0):
                    kv_copy(d, i, which).wait_send()
    if back >= 2:
        @pl.when(relays)
        def _():
            for which in range(2):
                relay_copy(G - 1, which).wait_send()
    if swap:
        @pl.when(inner)
        def _():
            if back >= 2:
                @pl.when(hands_on)
                def _():
                    for which in range(2):
                        for b in range(G):
                            hand_copy(b, which).wait_send()

            @pl.when(serves)
            def _():
                cross_q().wait_send()

            for which in range(2):
                cross_kv(which).wait_send()
                for d in range(back + 1):
                    @pl.when(passes(d))
                    def _():
                        pass_copy(d, which).wait_send()

    def end_send(u, carry):
        for j in range(per_blk):
            mine, remote, local = out_copy(u, j)

            @pl.when(jnp.logical_not(mine))
            def _():
                remote.wait_send()
        return carry

    lax.fori_loop(0, units, end_send, 0)

    pltpu.make_async_copy(out_ref, out_ref, orecv.at[0]).wait()


def solution(mesh):
    n_srv, n_head = mesh.shape["srv"], mesh.shape["head"]

    def body(queries, key_value_pair, lengths):
        tok, qw = queries.shape
        kv_all = key_value_pair.shape[2] // HEAD
        G = 2 if kv_all % 2 == 0 and n_srv % 2 == 0 else 1
        kvh = kv_all // G
        per = qw // HEAD // kv_all
        grp = G * tok
        n_grp = n_srv // G
        back = n_grp // 2
        T = tok // n_head
        R = max(tok // 2, T)
        chunk = per // 4
        ndoc = lengths.shape[0]
        heads = kvh * per
        nch = heads // chunk
        units = (grp // R) * nch
        W = back * grp + R
        swap = True and G == 2 and n_head % 2 == 0 and tok // R == 2
        cfg = (n_srv, n_head, G, back, tok, kvh, per, R, chunk, ndoc, swap)
        bf = jnp.bfloat16
        dma = pltpu.SemaphoreType.DMA
        return pl.pallas_call(
            functools.partial(kernel, cfg),
            out_shape=pltpu.VMEM((T, qw * n_head), bf),
            in_specs=[
                pl.BlockSpec(memory_space=pltpu.SMEM),
                pl.BlockSpec(memory_space=pl.ANY),
                pl.BlockSpec(memory_space=pl.ANY),
            ],
            out_specs=pl.BlockSpec(memory_space=pl.ANY),
            scratch_shapes=[
                pltpu.VMEM((G, tok // R, R, heads * HEAD), bf),
                pltpu.VMEM((heads, grp, HEAD), bf),
                pltpu.VMEM((2, 2, (back + 1) * grp, kvh * HEAD), bf),
                pltpu.VMEM((2, tok, kv_all * HEAD), bf),
                pltpu.VMEM((tok, kv_all * HEAD), bf),
                pltpu.VMEM((2, tok, kvh * HEAD), bf),
                pltpu.VMEM((G, 2, tok, HEAD), jnp.float32),
                pltpu.VMEM((R, W), jnp.float32),
                pltpu.VMEM((chunk * R, W), jnp.float32),
                pltpu.VMEM((chunk * R, HEAD), jnp.float32),
                pltpu.VMEM((units, R, chunk * HEAD), bf),
                dma((2,)),
                dma((G, tok // R)),
                dma((G, tok // R)),
                dma((back + 1, G, 2)),
                dma((back + 1, G, 2)),
                dma((G, 2)),
                dma((3,)),
                dma((2,)),
                dma((back + 1, 2)),
                dma((back + 1, G, 2)),
                dma((G, 2)),
                pltpu.SemaphoreType.REGULAR,
                dma((units * (R // T),)),
                dma((1,)),
            ],
            compiler_params=pltpu.CompilerParams(collective_id=0, has_side_effects=True),
            name="attend",
        )(lengths, queries, key_value_pair)

    in_specs = (P("srv", "head"), P(None, "srv", "head"), P())
    out_specs = P(("srv", "head"), None)
    return jax.shard_map(body, mesh=mesh, in_specs=in_specs, out_specs=out_specs, check_vma=False)
```
